32 devices in a mesh: wide: 8 (over y, x, core), narrow: 4 (over z).
Axes of the slice: x: 2, y: 2, z: 4, core: 2. Of those that a mesh axis runs over, the one named last changes fastest.
Arguments:
- fraction: float32 [3, 32768], P(None, ('wide', 'narrow')), may hold values from 0 to 1
- masses: float32 [32768], P(('wide', 'narrow')), may hold values from 0.05 to 0.5
- leaf_cell: int32 [3, 256], P(None, ('wide', 'narrow')), may hold values from 0 to 255, as said below
- exports: int32 [4, 64], P(None, ('wide', 'narrow')), may hold values from 0 to 8, as said below
- tile_lists: int32 [2, 256], P(None, ('wide', 'narrow')), may hold values from 0 to 7, as said below
Outputs:
- accel: float32 [3, 32768], P(None, ('wide', 'narrow'))
The draws below stay inside these ranges and needn't reach their ends.
Inputs may be any that keep to these rules, and one draw needn't show every extreme that they name: `leaf_cell`: column n belongs to rank m = n // 8, with wide index m // 4 and narrow index m mod 4: its first entry plus 0 .. 1 lies within that wide index's 32 planes, its second entry plus 0 .. 3 within that narrow index's 64 planes; the third entry is any cell. `exports`: row f and the 2 columns of rank m list distinct local leaf numbers of rank m to be exported across face f, then the value 8 in empty slots; every rank fills all slots of one of its rows. `tile_lists`: column n lists 2 distinct local leaf numbers of rank n // 8.
All inputs are finite; a program needn't handle non-finite values.
Results may differ from the reference program's by a relative error of at most 0.0003.
Values sent between devices are 32-bit elements; how exact they have to be, the bound alone decides.
A program may use at most 64 MiB of HBM per device.

```python
import math
import jax
import jax.numpy as jnp
from jax import lax

G = 256
LEAF = 128
PX = 2
PY = 4
PZ = 16
TILES = 2
LEAVES_DEV = 8
EXPORTS = 2
SLAB_X = 32
SLAB_Y = 64
COLUMNS = 4
RANKS = 32
PARTICLES = 32768
N_WIDE = 8
N_NARROW = 4


def layout(key):

    def per_rank(rank_index):
        subkeys = jax.random.split(jax.random.fold_in(key, rank_index), 6)
        slot_index = jnp.arange(LEAVES_DEV, dtype=jnp.int32)
        order_x = jax.random.permutation(subkeys[0], LEAVES_DEV).astype(jnp.int32)
        order_y = jax.random.permutation(subkeys[1], LEAVES_DEV).astype(jnp.int32)
        counts = jax.random.randint(subkeys[2], (4,), 1, EXPORTS + 1, dtype=jnp.int32)
        counts = jnp.where(jnp.arange(4, dtype=jnp.int32) == rank_index % 4, EXPORTS, counts)
        place_x = jnp.zeros((LEAVES_DEV,), jnp.int32).at[order_x].set(slot_index)
        place_y = jnp.zeros((LEAVES_DEV,), jnp.int32).at[order_y].set(slot_index)
        inner_x = jax.random.randint(subkeys[3], (LEAVES_DEV,), 1, SLAB_X - PX, dtype=jnp.int32)
        inner_y = jax.random.randint(subkeys[4], (LEAVES_DEV,), 1, SLAB_Y - PY, dtype=jnp.int32)
        base_x = jnp.where(place_x < counts[0], SLAB_X - PX, jnp.where((place_x >= EXPORTS) & (place_x < EXPORTS + counts[1]), 0, inner_x))
        base_y = jnp.where(place_y < counts[2], SLAB_Y - PY, jnp.where((place_y >= EXPORTS) & (place_y < EXPORTS + counts[3]), 0, inner_y))
        spacing = G // LEAVES_DEV
        base_z = slot_index * spacing + jax.random.randint(subkeys[5], (LEAVES_DEV,), 0, spacing, dtype=jnp.int32)
        wide_at = rank_index // COLUMNS
        narrow_at = rank_index % COLUMNS
        cell_table = jnp.stack([wide_at * SLAB_X + base_x, narrow_at * SLAB_Y + base_y, base_z]).astype(jnp.int32)
        column = jnp.arange(EXPORTS, dtype=jnp.int32)
        export_lists = jnp.stack([jnp.where(column < counts[0], order_x[column], LEAVES_DEV), jnp.where(column < counts[1], order_x[EXPORTS + column], LEAVES_DEV), jnp.where(column < counts[2], order_y[column], LEAVES_DEV), jnp.where(column < counts[3], order_y[EXPORTS + column], LEAVES_DEV)]).astype(jnp.int32)
        return (cell_table, export_lists)
    cell_table, export_lists = jax.vmap(per_rank)(jnp.arange(RANKS, dtype=jnp.int32))
    return (jnp.transpose(cell_table, (1, 0, 2)).reshape(3, -1), jnp.transpose(export_lists, (1, 0, 2)).reshape(4, -1))


def draw_leaf_cell(key, part):
    return layout(key)[0]


def draw_exports(key, part):
    return layout(key)[1]


def draw_tile_lists(key, part):
    leaf_total = RANKS * LEAVES_DEV
    subkeys = jax.random.split(jax.random.fold_in(key, 7), leaf_total)
    chosen = jax.vmap(lambda subkey: jax.random.permutation(subkey, TILES + 1)[:TILES])(subkeys).astype(jnp.int32)
    leaf_index = jnp.arange(leaf_total, dtype=jnp.int32) % LEAVES_DEV
    local_ids = (leaf_index[:, None] + chosen - TILES // 2) % LEAVES_DEV
    return jnp.transpose(local_ids).astype(jnp.int32)


def shard_levels(own_key, shape, cuts, low, top_value):
    level = 1.0
    for axis_at, parts in cuts:
        heights = jax.random.uniform(jax.random.fold_in(jax.random.fold_in(own_key, 6), axis_at), (parts,), jnp.float32, low / len(cuts), top_value / len(cuts))
        level = level * jnp.repeat(jnp.exp(heights), shape[axis_at] // parts).reshape((-1,) + (1,) * (len(shape) - 1 - axis_at))
    return level


def setup_inputs(seed: int = 0) -> dict:
    streams_of = jax.random.split(jax.random.key(seed), 6)
    return {
        "fraction": jnp.clip(1.0 * jax.random.uniform(streams_of[0], (3, PARTICLES), jnp.float32) ** shard_levels(streams_of[0], (3, PARTICLES), ((1, 32),), -0.2, 0.2), 0.0, 1.0),
        "masses": jnp.clip(jnp.exp(math.log(0.5) - 2.3025851 * jax.random.uniform(streams_of[1], (PARTICLES,), jnp.float32) ** shard_levels(streams_of[1], (PARTICLES,), ((0, 32),), -0.2, 0.2)), 0.05, 0.5),
        "leaf_cell": draw_leaf_cell(jax.random.fold_in(streams_of[5], 71), 0),
        "exports": draw_exports(jax.random.fold_in(streams_of[5], 71), 0),
        "tile_lists": draw_tile_lists(jax.random.fold_in(streams_of[5], 71), 0),
    }


SCREEN = 0.5
SOFTEN = 0.5
PRECISE = lax.Precision.HIGHEST

def cic_weights(fraction, extent):
    coordinate = 0.5 + fraction * (extent - 1.0)
    centres = jnp.arange(extent, dtype=jnp.int32).astype(jnp.float32) + 0.5
    return jnp.maximum(0.0, 1.0 - jnp.abs(coordinate[..., None] - centres))

def leaf_positions(cell_table, fraction):
    leaf_total = cell_table.shape[1]
    extents = jnp.asarray([PX - 1.0, PY - 1.0, PZ - 1.0], dtype=jnp.float32)
    scaled = fraction.reshape(3, leaf_total, -1) * extents[:, None, None] + 0.5
    return jnp.transpose(cell_table.astype(jnp.float32)[:, :, None] + scaled, (1, 0, 2))

def tile_block(targets, sources, masses):
    separation = sources[:, :, :, None, :] - targets[:, None, :, :, None]
    separation = separation - G * jnp.floor(separation / G + 0.5)
    squared = lax.optimization_barrier(jnp.sum(separation * separation, axis=2))
    distance = jnp.sqrt(squared)
    screened = jax.scipy.special.erfc(distance / (2.0 * SCREEN)) + distance / (SCREEN * math.sqrt(math.pi)) * jnp.exp(-squared / (4.0 * SCREEN * SCREEN))
    weight = masses[:, :, None, :] * screened / (squared + SOFTEN * SOFTEN) ** 1.5
    return lax.optimization_barrier(jnp.sum(weight[:, :, None, :, :] * separation, axis=(1, 4)))

def tile_forces(targets, sources, masses):
    block_size = 4
    blocks = targets.shape[0] // block_size

    def one_block(blocked):
        return tile_block(blocked[0], blocked[1], blocked[2])
    result = lax.map(one_block, (targets.reshape((blocks, block_size) + targets.shape[1:]), sources.reshape((blocks, block_size) + sources.shape[1:]), masses.reshape((blocks, block_size) + masses.shape[1:])))
    return result.reshape(targets.shape)

def green_factor(wave_x, wave_y, wave_z):
    squared_sum = 0.0
    for wavenumber in (wave_x, wave_y, wave_z):
        folded = jnp.where(wavenumber > G // 2, wavenumber - G, wavenumber).astype(jnp.float32) * (2.0 * math.pi / G)
        squared_sum = squared_sum + folded * folded
    divisor = jnp.where(squared_sum > 0, squared_sum, 1.0)
    return jnp.where(squared_sum > 0, -4.0 * math.pi * jnp.exp(-squared_sum * SCREEN * SCREEN) / divisor, 0.0)

def differences(potential, axis_index):
    return -(8.0 * (jnp.roll(potential, -1, axis_index) - jnp.roll(potential, 1, axis_index)) - (jnp.roll(potential, -2, axis_index) - jnp.roll(potential, 2, axis_index))) / 12.0

def reference(fraction, masses, leaf_cell, exports, tile_lists):
    ranks = leaf_cell.shape[1] // LEAVES_DEV
    positions = leaf_positions(leaf_cell, fraction)
    leaf_mass = masses.reshape(-1, LEAF)
    cell_x = leaf_cell[0][:, None] + jnp.arange(PX, dtype=jnp.int32)
    cell_y = leaf_cell[1][:, None] + jnp.arange(PY, dtype=jnp.int32)
    cell_z = (leaf_cell[2][:, None] + jnp.arange(PZ, dtype=jnp.int32)) % G
    fraction_leaf = fraction.reshape(3, -1, LEAF)
    weight_x = cic_weights(fraction_leaf[0], PX)
    weight_y = cic_weights(fraction_leaf[1], PY)
    weight_z = cic_weights(fraction_leaf[2], PZ)
    patch_mass = jnp.einsum('np,npa,npb,npc->nabc', leaf_mass, weight_x, weight_y, weight_z, precision=PRECISE)
    density = jnp.zeros((G, G, G), jnp.float32).at[cell_x[:, :, None, None], cell_y[:, None, :, None], cell_z[:, None, None, :]].add(patch_mass)
    spectrum = jnp.fft.fftn(density)
    waves = jnp.arange(G, dtype=jnp.int32)
    greens = green_factor(waves[:, None, None], waves[None, :, None], waves[None, None, :])
    potential = jnp.real(jnp.fft.ifftn(spectrum * greens))
    accel_field = jnp.stack([differences(potential, 0), differences(potential, 1), differences(potential, 2)])
    sampled = accel_field[:, cell_x[:, :, None, None], cell_y[:, None, :, None], cell_z[:, None, None, :]]
    long_range = jnp.einsum('knabc,npa,npb,npc->knp', sampled, weight_x, weight_y, weight_z, precision=PRECISE)
    by_rank = positions.reshape(ranks, LEAVES_DEV, 3, LEAF)
    mass_rank = leaf_mass.reshape(ranks, LEAVES_DEV, LEAF)
    lists_rank = jnp.transpose(tile_lists.reshape(TILES, ranks, LEAVES_DEV), (1, 2, 0))
    export_rank = jnp.transpose(exports.reshape(4, ranks, EXPORTS), (1, 0, 2))

    def per_rank(rank_index):
        own_leaves = by_rank[rank_index]
        own_mass = mass_rank[rank_index]
        own_lists = lists_rank[rank_index]
        result = tile_forces(own_leaves, own_leaves[own_lists], own_mass[own_lists])
        wide_at = rank_index // N_NARROW
        narrow_at = rank_index % N_NARROW
        neighbours = jnp.stack([(wide_at + 1) % N_WIDE * N_NARROW + narrow_at, (wide_at - 1) % N_WIDE * N_NARROW + narrow_at, wide_at * N_NARROW + (narrow_at + 1) % N_NARROW, wide_at * N_NARROW + (narrow_at - 1) % N_NARROW]).astype(jnp.int32)
        listed = export_rank[rank_index]
        chosen = jnp.minimum(listed, LEAVES_DEV - 1)
        filled = (listed < LEAVES_DEV).astype(jnp.float32)
        guest_lists = lists_rank[neighbours[:, None], chosen]
        sources = by_rank[neighbours[:, None, None], guest_lists]
        source_mass = mass_rank[neighbours[:, None, None], guest_lists]
        guests = own_leaves[chosen]
        forces = tile_forces(guests.reshape(4 * EXPORTS, 3, LEAF), sources.reshape(4 * EXPORTS, TILES, 3, LEAF), source_mass.reshape(4 * EXPORTS, TILES, LEAF))
        forces = forces.reshape(4, EXPORTS, 3, LEAF) * filled[:, :, None, None]
        return result.at[chosen.reshape(-1)].add(forces.reshape(4 * EXPORTS, 3, LEAF))
    short_range = lax.map(per_rank, jnp.arange(ranks, dtype=jnp.int32))
    short_range = jnp.transpose(short_range, (2, 0, 1, 3)).reshape(3, -1, LEAF)
    return (long_range + short_range).reshape(3, -1)
```

```python
import functools
import math

import jax
import jax.numpy as jnp
from jax import lax
from jax.experimental import pallas as pl
from jax.experimental.pallas import tpu as pltpu
from jax.sharding import PartitionSpec as P

G = 256
PX = 2
PY = 4
PZ = 16
AB = PX * PY
SCREEN = 0.5
SOFTEN = 0.5
ERFCX = (
    0.2820947416810428,
    0.28210427504184366,
    0.24651391069954823,
    0.18039116519942175,
    0.058372405908860704,
    0.0792320361696661,
    -0.1983246779625943,
    0.030722780905291756,
    0.06437369661731697,
    -0.025480486181070308,
)
VMEM = pl.BlockSpec(memory_space=pltpu.VMEM)
SMEM = pl.BlockSpec(memory_space=pltpu.SMEM)


def iota(shape, dim):
    return lax.broadcasted_iota(jnp.int32, shape, dim)


def sincos(count):
    quarters = count * (4.0 / G)
    near = jnp.floor(quarters + 0.5)
    z = (quarters - near) * (math.pi / 2)
    q = near.astype(jnp.int32)
    zz = z * z
    c = 1.0 + zz * (-0.5 + zz * (1.0 / 24 + zz * (-1.0 / 720 + zz * (1.0 / 40320))))
    s = z * (1.0 + zz * (-1.0 / 6 + zz * (1.0 / 120 + zz * (-1.0 / 5040))))
    swap = (q & 1) == 1
    cosine = jnp.where(swap, s, c)
    sine = jnp.where(swap, c, s)
    cosine = jnp.where(((q + 1) & 2) == 2, -cosine, cosine)
    sine = jnp.where((q & 2) == 2, -sine, sine)
    return cosine, sine


def split(x):
    hi = x.astype(jnp.bfloat16)
    return hi, (x - hi.astype(jnp.float32)).astype(jnp.bfloat16)


def dot3(left, right, dims=((1,), (0,))):
    dims = (dims, ((), ()))
    dot = functools.partial(
        lax.dot_general, dimension_numbers=dims, preferred_element_type=jnp.float32
    )
    return dot(left[0], right[0]) + (dot(left[0], right[1]) + dot(left[1], right[0]))


def slope(wave):
    w = wave.astype(jnp.float32)
    return (8.0 * sincos(w)[1] - sincos(2.0 * w)[1]) * (1.0 / 6.0)


def real_mode(index, count):
    half = count // 2
    wave = index // count * half + index % half
    second = (index % count) // half
    top = (second == 1) & (wave == 0)
    sine = (second == 1) & (wave > 0)
    return jnp.where(top, G // 2, wave), sine


def share(wave):
    return jnp.where(wave % (G // 2) == 0, 1.0, 2.0)


def device(rank):
    columns = lax.axis_size("narrow")
    return {"wide": lax.div(rank, columns), "narrow": lax.rem(rank, columns)}


def remote(src, dst, send, recv, to):
    return pltpu.make_async_remote_copy(
        src_ref=src,
        dst_ref=dst,
        send_sem=send,
        recv_sem=recv,
        device_id=to,
        device_id_type=pl.DeviceIdType.MESH,
    )


def axis_tables(position, waves, first, steps):
    rows = waves
    row = iota((rows, 1), 0)
    wave = first + row
    c, s = sincos(wave.astype(jnp.float32) * position)
    turn_c, turn_s = sincos(wave.astype(jnp.float32))
    tilt = slope(wave)
    alternate = 1.0 - 2.0 * (position.astype(jnp.int32) & 1).astype(jnp.float32)
    top = wave == 0
    values, slopes = [], []
    for b in range(steps):
        if b:
            c, s = c * turn_c - s * turn_s, s * turn_c + c * turn_s
            alternate = -alternate
        values.append((c, jnp.where(top, alternate, s)))
        slopes.append((tilt * s, -(tilt * c)))
    return values, slopes


def pair_job(job, rank, target, leaf_cell, books, forces):
    members = books.shape[3]
    leaves = books.shape[2]
    leaf = iota((leaves, members), 0).astype(jnp.float32)
    lane = iota((1, members), 1)
    tgt = [books[0, c, pl.ds(target, 1), :] for c in range(3)]
    origin = [leaf_cell[c, target].astype(jnp.float32) for c in range(3)]
    lists = books[rank, 4, pl.ds(target, 1), :]
    swapped = pltpu.roll(lists, members // 2, 1)
    total = [0.0, 0.0, 0.0]
    for k in range(2):
        wanted = jnp.where((lane < members // 2) == (k == 0), lists, swapped)
        mine = leaf == wanted
        rows = []
        for c in range(4):
            row = jnp.sum(jnp.where(mine, books[rank, c], 0.0), axis=0, keepdims=True)
            if c < 3:
                row = row - G * jnp.floor((row - origin[c]) * (1.0 / G) + 0.5)
            rows.append(row)
        cols = jnp.concatenate(rows + [jnp.zeros((4, members), jnp.float32)], axis=0).T
        d = [
            jnp.broadcast_to(cols[:, c : c + 1], (members, members)) - tgt[c] for c in range(3)
        ]
        squared = d[0] * d[0] + d[1] * d[1] + d[2] * d[2]
        r = squared * lax.rsqrt(jnp.maximum(squared, 1e-30))
        t = 1.0 / (1.0 + 0.5 * r)
        poly = ERFCX[-1] * t + ERFCX[-2]
        for coefficient in ERFCX[-3::-1]:
            poly = poly * t + coefficient
        screened = jnp.exp(-squared) * (poly * t + (2.0 / math.sqrt(math.pi)) * r)
        inv = lax.rsqrt(squared + SOFTEN * SOFTEN)
        w = cols[:, 3:4] * screened * (inv * inv * inv)
        for c in range(3):
            total[c] = total[c] + jnp.sum(w * d[c], axis=0, keepdims=True)
    forces[job] = jnp.concatenate(total + [jnp.zeros((5, members), jnp.float32)], axis=0)


def kernel(
    zg,
    yg,
    leaf_cell,
    exports,
    tile_lists,
    fraction,
    masses,
    out,
    zt,
    recv,
    books,
    green,
    ee_hi,
    ee_lo,
    values,
    slopes,
    spectrum,
    pairs,
    lones,
    back_pairs,
    back_lones,
    forces,
    wz_hi,
    wz_lo,
    basis,
    lone_basis,
    planar,
    near_send,
    near_recv,
    sends,
    recvs,
):
    n_wide, n_narrow = lax.axis_size("wide"), lax.axis_size("narrow")
    ranks = n_wide * n_narrow
    leaves = leaf_cell.shape[1]
    slots = exports.shape[1]
    members = books.shape[3]
    nkz = G // zg
    nky = G // yg
    half_z = nkz // 2
    half = G // 2
    w, v = lax.axis_index("wide"), lax.axis_index("narrow")
    me = w * n_narrow + v
    my_z, my_y = lax.rem(me, zg), lax.div(me, zg)
    f32 = jnp.float32

    barrier = pltpu.get_barrier_semaphore()

    def greet(i, carry):
        pl.semaphore_signal(
            barrier,
            inc=1,
            device_id=device(lax.rem(me + i, ranks)),
            device_id_type=pl.DeviceIdType.MESH,
        )
        return carry

    lax.fori_loop(1, ranks, greet, 0)

    leaf_row = iota((leaves, members), 0)
    lane = iota((1, members), 1)
    for c, extent in enumerate((PX, PY, PZ)):
        cell = jnp.zeros((leaves, members), f32)
        for n in range(leaves):
            cell = jnp.where(leaf_row == n, leaf_cell[c, n].astype(f32), cell)
        u = jnp.concatenate(
            [fraction[c : c + 1, n * members : (n + 1) * members] for n in range(leaves)], axis=0
        )
        books[0, c] = cell + (u * (extent - 1.0) + 0.5)
    books[0, 3] = jnp.concatenate(
        [masses[:, n * members : (n + 1) * members] for n in range(leaves)], axis=0
    )
    lists = jnp.zeros((leaves, members), f32)
    for n in range(leaves):
        both = jnp.where(
            lane < members // 2, tile_lists[0, n].astype(f32), tile_lists[1, n].astype(f32)
        )
        lists = jnp.where(leaf_row == n, both, lists)
    books[0, 4] = lists

    particles = leaves * members
    patch_row = iota((AB, particles), 0)
    planar_weights = None
    for c, extent, index in ((0, PX, patch_row // PY), (1, PY, patch_row % PY)):
        coordinate = 0.5 + fraction[c : c + 1, :] * (extent - 1.0)
        part = jnp.maximum(0.0, 1.0 - jnp.abs(coordinate - (index.astype(f32) + 0.5)))
        planar_weights = part if planar_weights is None else planar_weights * part
    planar[...] = planar_weights
    coordinate = 0.5 + fraction[2:3, :] * (PZ - 1.0)
    deep = jnp.maximum(
        0.0, 1.0 - jnp.abs(coordinate - (iota((PZ, particles), 0).astype(f32) + 0.5))
    )
    deep_hi, deep_lo = split(deep)
    wz_hi[...] = jnp.zeros_like(wz_hi)
    wz_lo[...] = jnp.zeros_like(wz_lo)
    for n in range(leaves):
        at = slice(n * members, (n + 1) * members)
        wz_hi[n * PZ : (n + 1) * PZ, at] = deep_hi[:, at]
        wz_lo[n * PZ : (n + 1) * PZ, at] = deep_lo[:, at]
    weighted = jnp.concatenate(
        [planar_weights * masses[...], jnp.zeros((PZ - AB, particles), f32)], axis=0
    )
    weighted = split(jnp.concatenate([weighted] * leaves, axis=0))
    width = leaves * PZ
    patches = dot3((wz_hi[...], wz_lo[...]), weighted, ((1,), (1,)))
    same = iota((width, width), 0) // PZ == iota((width, width), 1) // PZ
    patches = split(jnp.where(same, patches, 0.0))

    column = iota((1, width), 1)
    notes = []
    for c in range(3):
        note = jnp.zeros((1, width), f32)
        for n in range(leaves):
            note = jnp.where(column // PZ == n, leaf_cell[c, n].astype(f32), note)
        notes.append(note)
    wave, sine = real_mode(iota((G, 1), 0), nkz)
    place = notes[2] + (column % PZ).astype(f32)
    phi = sincos(wave.astype(f32) * place - jnp.where(sine, float(G // 4), 0.0))[0]
    phi = split(phi)
    basis[0], basis[1] = phi
    row = iota((half, 1), 0)
    for part in range(2):
        turn = float(part * (G // 4))
        psi = split(sincos(row.astype(f32) * place - turn)[1] * slope(row))
        lone_basis[2 * part], lone_basis[2 * part + 1] = psi
    flat = dot3(phi, patches)
    zt[...] = jnp.where(
        column % PZ == AB, notes[0], jnp.where(column % PZ == AB + 1, notes[1], flat)
    )

    pl.semaphore_wait(barrier, ranks - 1)

    def send_out(i, carry):
        to = lax.rem(me + i, ranks)
        remote(
            zt.at[pl.ds(pl.multiple_of(lax.rem(to, zg) * nkz, 8), nkz), :],
            recv.at[pl.ds(pl.multiple_of(me * nkz, 8), nkz), :],
            sends.at[0],
            recvs.at[0],
            device(to),
        ).start()
        return carry

    lax.fori_loop(1, ranks, send_out, 0)
    near = []
    for face, to in enumerate(
        (
            {"wide": lax.rem(w + n_wide - 1, n_wide), "narrow": v},
            {"wide": lax.rem(w + 1, n_wide), "narrow": v},
            {"wide": w, "narrow": lax.rem(v + n_narrow - 1, n_narrow)},
            {"wide": w, "narrow": lax.rem(v + 1, n_narrow)},
        )
    ):
        near.append(
            remote(books.at[0], books.at[face + 1], near_send.at[face], near_recv.at[face], to)
        )
    for copy in near:
        copy.start()

    recv[pl.ds(pl.multiple_of(me * nkz, 8), nkz), :] = zt[
        pl.ds(pl.multiple_of(my_z * nkz, 8), nkz), :
    ]

    unit = 2.0 * math.pi / G
    half_y = nky // 2
    first_y = my_y * half_y
    wave_x, _ = real_mode(iota((1, G), 1), G)
    index_y = iota((nky, 1), 0)
    wave_y = first_y + index_y % half_y
    wave_y = jnp.where((wave_y == 0) & (index_y >= half_y), half, wave_y)
    kx = wave_x.astype(f32) * unit
    ky = wave_y.astype(f32) * unit
    plane = kx * kx + ky * ky
    top = jnp.exp(-plane * (SCREEN * SCREEN)) * (share(wave_x) * share(wave_y))

    def fill_green(j, carry):
        wave_z, _ = real_mode(jnp.full((1, 1), my_z * nkz + j, jnp.int32), nkz)
        kz = wave_z.astype(f32) * unit
        kz2 = kz * kz
        scale = jnp.exp(-kz2 * (SCREEN * SCREEN)) * share(wave_z) * (-4.0 * math.pi / G**3)
        total = plane + kz2
        green[j] = jnp.where(total > 0, top * scale / jnp.where(total > 0, total, 1.0), 0.0)
        return carry

    lax.fori_loop(0, nkz, fill_green, 0)

    def own(n, carry):
        pair_job(n, 0, n, leaf_cell, books, forces)
        return carry

    lax.fori_loop(0, leaves, own, 0)

    def received(i, buffer, rows):
        whole = buffer.at[pl.ds(0, (ranks - 1) * rows), :]
        return remote(
            whole, whole, sends.at[i], recvs.at[i], device(lax.rem(me + 1, ranks))
        )

    received(0, recv, nkz).wait_recv()

    group = min(ranks, G // leaves)
    blocks = ranks // group
    cols = group * leaves

    def gathered(block, j):
        got = recv[pl.ds(block * group * nkz + j, group, nkz), :]
        return got.T

    def folded(turned, start):
        return jnp.concatenate(
            [turned[n * PZ + start : n * PZ + start + 8, :] for n in range(leaves)], axis=1
        )

    def tables(block):
        place = folded(gathered(block, 0), AB)
        value, tilt = axis_tables(place[0:1, :], half, 0, PX)
        for a in range(PX):
            for kind, table in enumerate((value[a], tilt[a])):
                at = slice((kind * PX + a) * cols, (kind * PX + a + 1) * cols)
                for part in range(2):
                    hi, lo = split(table[part])
                    ee_hi[part * half : (part + 1) * half, at] = hi
                    ee_lo[part * half : (part + 1) * half, at] = lo
        value, tilt = axis_tables(place[1:2, :], half_y, first_y, PY)
        for b in range(PY):
            for part in range(2):
                values[b, part * half_y : (part + 1) * half_y, :] = value[b][part]
                slopes[b, part * half_y : (part + 1) * half_y, :] = tilt[b][part]

    def forward(block, j):
        rows = folded(gathered(block, j), 0)
        halves = []
        for a in range(PX):
            m = rows[a * PY : a * PY + 1, :] * values[0]
            for b in range(1, PY):
                m = m + rows[a * PY + b : a * PY + b + 1, :] * values[b]
            halves.append(m)
        m = split(jnp.concatenate(halves, axis=1))
        at = slice(0, PX * cols)
        return dot3(m, (ee_hi[:, at], ee_lo[:, at]), ((1,), (1,)))

    def inverse(block, j, qs):
        alone = []
        for part, q in enumerate(qs):
            field = dot3(split(q), (ee_hi[...], ee_lo[...]))
            slabs = []
            for kind, table in ((1, values), (0, slopes), (0, values)):
                rows = []
                for a in range(PX):
                    at = (kind * PX + a) * cols
                    u = field[:, at : at + cols]
                    for b in range(PY):
                        rows.append(jnp.sum(u * table[b], axis=0, keepdims=True))
                slabs.append(jnp.concatenate(rows, axis=0))
            pair = jnp.concatenate(slabs[:2], axis=0)
            pair = jnp.concatenate(
                [pair[:, n * group : (n + 1) * group] for n in range(leaves)], axis=0
            )
            alone += [slabs[2][:, n * group : (n + 1) * group] for n in range(leaves)]
            at = pl.ds(block * group * nkz + part * half_z + j, group, nkz)
            pairs[at, :] = pair.T
        at = pl.ds(block * group * half_z + j, group, half_z)
        lones[at, :] = jnp.concatenate(alone, axis=0).T

    if blocks == 1:
        tables(0)

        def both(j, carry):
            inverse(
                0,
                j,
                [forward(0, i) * green[i] for i in (j, half_z + j)],
            )
            return carry

        lax.fori_loop(0, half_z, both, 0)
    else:
        spectrum[...] = jnp.zeros_like(spectrum)

        def forth(block, carry):
            tables(block)

            def step(j, carry):
                spectrum[j] += forward(block, j)
                return carry

            return lax.fori_loop(0, nkz, step, carry)

        lax.fori_loop(0, blocks, forth, 0)

        def reverse(block, carry):
            tables(block)

            def step(j, carry):
                inverse(block, j, [spectrum[i] * green[i] for i in (j, half_z + j)])
                return carry

            return lax.fori_loop(0, half_z, step, carry)

        lax.fori_loop(0, blocks, reverse, 0)

    def slot(rank, rows):
        return pl.ds(pl.multiple_of(rank * rows, rows), rows)

    def send_back(i, carry):
        to = lax.rem(me + i, ranks)
        for n, (src, dst, rows) in enumerate(
            ((pairs, back_pairs, nkz), (lones, back_lones, half_z))
        ):
            remote(
                src.at[slot(to, rows), :],
                dst.at[slot(me, rows), :],
                sends.at[2 + n],
                recvs.at[2 + n],
                device(to),
            ).start()
        return carry

    lax.fori_loop(1, ranks, send_back, 0)
    back_pairs[slot(me, nkz), :] = pairs[slot(me, nkz), :]
    back_lones[slot(me, half_z), :] = lones[slot(me, half_z), :]

    for copy in near:
        copy.wait_recv()

    def guest(j, carry):
        face = j // slots
        target = jnp.minimum(exports[face, j % slots], leaves - 1)
        pair_job(leaves + j, face + 1, target, leaf_cell, books, forces)
        return carry

    lax.fori_loop(0, 4 * slots, guest, 0)
    short = []
    for n in range(leaves):
        force = forces[n]
        for j in range(4 * slots):
            mine_too = jnp.where(exports[j // slots, j % slots] == n, 1.0, 0.0)
            force = force + forces[leaves + j] * mine_too
        short.append(force)
    short = jnp.concatenate(short, axis=1)

    received(2, back_pairs, nkz).wait_recv()
    received(3, back_lones, half_z).wait_recv()

    def summed(buffer, rows):
        total = buffer[0:rows, :]
        for part in range(1, yg):
            total = total + buffer[part * rows : (part + 1) * rows, :]
        return split(total)

    def own_part(table, start, rows):
        kept = jnp.where(column // PZ == 0, table[start : start + rows, :], 0.0)
        for n in range(1, leaves):
            at = start + n * rows
            kept = kept + jnp.where(column // PZ == n, table[at : at + rows, :], 0.0)
        return kept

    along = dot3(summed(back_pairs, G), (basis[0], basis[1]), ((0,), (0,)))
    sampled = [own_part(along, 0, PZ)]
    lone = summed(back_lones, half)
    deep = None
    for part in range(2):
        rows = dot3(lone, (lone_basis[2 * part], lone_basis[2 * part + 1]), ((0,), (0,)))
        rows = own_part(rows, part * leaves * AB, AB)
        deep = rows if deep is None else deep + rows
    sampled.append(deep)
    sampled = jnp.concatenate(sampled, axis=0)
    got = dot3(split(sampled), (wz_hi[...], wz_lo[...]))
    for c in range(3):
        out[c : c + 1, :] = (
            jnp.sum(got[c * AB : (c + 1) * AB, :] * planar[...], axis=0, keepdims=True)
            + short[c : c + 1, :]
        )
    for copy in near:
        copy.wait_send()
    received(0, recv, nkz).wait_send()
    received(2, back_pairs, nkz).wait_send()
    received(3, back_lones, half_z).wait_send()


def local(fraction, masses, leaf_cell, exports, tile_lists):
    leaves = leaf_cell.shape[1]
    members = masses.shape[0] // leaves
    slots = exports.shape[1]
    ranks = lax.axis_size("wide") * lax.axis_size("narrow")
    f32, bf16 = jnp.float32, jnp.bfloat16
    zg = min(ranks, G // 8)
    yg = ranks // zg
    nkz, nky = G // zg, G // yg
    group = min(ranks, G // leaves)
    cols = group * leaves
    width = leaves * PZ
    blocks = ranks // group
    return pl.pallas_call(
        functools.partial(kernel, zg, yg),
        out_shape=jax.ShapeDtypeStruct((3, leaves * members), f32),
        in_specs=[SMEM, SMEM, SMEM, VMEM, VMEM],
        out_specs=VMEM,
        scratch_shapes=[
            pltpu.VMEM((G, width), f32),
            pltpu.VMEM((ranks * nkz, width), f32),
            pltpu.VMEM((5, 5, leaves, members), f32),
            pltpu.VMEM((nkz, nky, G), f32),
            pltpu.VMEM((G, 2 * PX * cols), bf16),
            pltpu.VMEM((G, 2 * PX * cols), bf16),
            pltpu.VMEM((PY, nky, cols), f32),
            pltpu.VMEM((PY, nky, cols), f32),
            pltpu.VMEM((nkz, nky, G) if blocks > 1 else (1, 8, 128), f32),
            pltpu.VMEM((ranks * nkz, width), f32),
            pltpu.VMEM((ranks * nkz // 2, width), f32),
            pltpu.VMEM((ranks * nkz, width), f32),
            pltpu.VMEM((ranks * nkz // 2, width), f32),
            pltpu.VMEM((leaves + 4 * slots, 8, members), f32),
            pltpu.VMEM((width, leaves * members), bf16),
            pltpu.VMEM((width, leaves * members), bf16),
            pltpu.VMEM((2, G, width), bf16),
            pltpu.VMEM((4, G // 2, width), bf16),
            pltpu.VMEM((AB, leaves * members), f32),
            pltpu.SemaphoreType.DMA((4,)),
            pltpu.SemaphoreType.DMA((4,)),
            pltpu.SemaphoreType.DMA((4,)),
            pltpu.SemaphoreType.DMA((4,)),
        ],
        compiler_params=pltpu.CompilerParams(
            collective_id=0, has_side_effects=True, vmem_limit_bytes=56 * 2**20
        ),
        name="treepm",
    )(leaf_cell, exports, tile_lists, fraction, masses.reshape(1, -1))


def solution(mesh):
    placed = (
        P(None, ("wide", "narrow")),
        P(("wide", "narrow")),
        P(None, ("wide", "narrow")),
        P(None, ("wide", "narrow")),
        P(None, ("wide", "narrow")),
    )
    return jax.shard_map(
        local, mesh=mesh, in_specs=placed, out_specs=P(None, ("wide", "narrow")), check_vma=False
    )
```

```python
import functools
import math

import jax
import jax.numpy as jnp
from jax import lax
from jax.experimental import pallas as pl
from jax.experimental.pallas import tpu as pltpu
from jax.sharding import PartitionSpec as P

G = 256
PX = 2
PY = 4
PZ = 16
AB = PX * PY
SLOT = 8
BACK = 16
CHUNK = 16
SCREEN = 0.5
SOFTEN = 0.5
ERFCX = (
    0.2820947416810428,
    0.28210427504184366,
    0.24651391069954823,
    0.18039116519942175,
    0.058372405908860704,
    0.0792320361696661,
    -0.1983246779625943,
    0.030722780905291756,
    0.06437369661731697,
    -0.025480486181070308,
)
VMEM = pl.BlockSpec(memory_space=pltpu.VMEM)
SMEM = pl.BlockSpec(memory_space=pltpu.SMEM)


def iota(shape, dim):
    return lax.broadcasted_iota(jnp.int32, shape, dim)


def sincos(count):
    quarters = count * (4.0 / G)
    near = jnp.floor(quarters + 0.5)
    z = (quarters - near) * (math.pi / 2)
    q = near.astype(jnp.int32)
    zz = z * z
    c = 1.0 + zz * (-0.5 + zz * (1.0 / 24 + zz * (-1.0 / 720 + zz * (1.0 / 40320))))
    s = z * (1.0 + zz * (-1.0 / 6 + zz * (1.0 / 120 + zz * (-1.0 / 5040))))
    swap = (q & 1) == 1
    cosine = jnp.where(swap, s, c)
    sine = jnp.where(swap, c, s)
    cosine = jnp.where(((q + 1) & 2) == 2, -cosine, cosine)
    sine = jnp.where((q & 2) == 2, -sine, sine)
    return cosine, sine


def split(x):
    hi = x.astype(jnp.bfloat16)
    return hi, (x - hi.astype(jnp.float32)).astype(jnp.bfloat16)


def dot3(left, right, dims=((1,), (0,))):
    dims = (dims, ((), ()))
    dot = functools.partial(
        lax.dot_general, dimension_numbers=dims, preferred_element_type=jnp.float32
    )
    return dot(left[0], right[0]) + (dot(left[0], right[1]) + dot(left[1], right[0]))


def slope(wave):
    w = wave.astype(jnp.float32)
    return (8.0 * sincos(w)[1] - sincos(2.0 * w)[1]) * (1.0 / 6.0)


def real_mode(index, count):
    half = count // 2
    wave = index // count * half + index % half
    second = (index % count) // half
    top = (second == 1) & (wave == 0)
    sine = (second == 1) & (wave > 0)
    return jnp.where(top, G // 2, wave), sine


def share(wave):
    return jnp.where(wave % (G // 2) == 0, 1.0, 2.0)


def each_peer(far, visit):
    n_wide, n_narrow = lax.axis_size("wide"), lax.axis_size("narrow")
    w, v = lax.axis_index("wide"), lax.axis_index("narrow")
    span = n_narrow // 2
    start = lax.rem(lax.div(v, span) + far, 2) * span
    columns = [start + lax.rem(lax.rem(v, span) + b, span) for b in range(span)]

    def row(at, first):
        for column in columns[first:]:
            visit(at, column, {"wide": at, "narrow": column})

    row(w, 1 - far)
    if n_wide <= 8:
        for a in range(1, n_wide):
            row(lax.rem(w + a, n_wide), 0)
    else:

        def step(a, carry):
            row(lax.rem(w + a, n_wide), 0)
            return carry

        lax.fori_loop(1, n_wide, step, 0)


def place_of(far, w, v):
    n_wide, n_narrow = lax.axis_size("wide"), lax.axis_size("narrow")
    span = n_narrow // 2
    return (far * n_wide + w) * span + lax.rem(v, span)


def remote(src, dst, send, recv, to):
    return pltpu.make_async_remote_copy(
        src_ref=src,
        dst_ref=dst,
        send_sem=send,
        recv_sem=recv,
        device_id=to,
        device_id_type=pl.DeviceIdType.MESH,
    )


def axis_tables(position, waves, first, steps):
    rows = waves
    row = iota((rows, 1), 0)
    wave = first + row
    c, s = sincos(wave.astype(jnp.float32) * position)
    turn_c, turn_s = sincos(wave.astype(jnp.float32))
    tilt = slope(wave)
    alternate = 1.0 - 2.0 * (position.astype(jnp.int32) & 1).astype(jnp.float32)
    top = wave == 0
    values, slopes = [], []
    for b in range(steps):
        if b:
            c, s = c * turn_c - s * turn_s, s * turn_c + c * turn_s
            alternate = -alternate
        values.append((c, jnp.where(top, alternate, s)))
        slopes.append((tilt * s, -(tilt * c)))
    return values, slopes


def pair_job(job, rank, target, leaf_cell, books, forces):
    members = books.shape[3]
    leaves = books.shape[2]
    leaf = iota((leaves, members), 0).astype(jnp.float32)
    lane = iota((1, members), 1)
    tgt = [books[0, c, pl.ds(target, 1), :] for c in range(3)]
    origin = [leaf_cell[c, target].astype(jnp.float32) for c in range(3)]
    lists = books[rank, 4, pl.ds(target, 1), :]
    swapped = pltpu.roll(lists, members // 2, 1)
    total = [0.0, 0.0, 0.0]
    for k in range(2):
        wanted = jnp.where((lane < members // 2) == (k == 0), lists, swapped)
        mine = leaf == wanted
        rows = []
        for c in range(4):
            row = jnp.sum(jnp.where(mine, books[rank, c], 0.0), axis=0, keepdims=True)
            if c < 3:
                row = row - G * jnp.floor((row - origin[c]) * (1.0 / G) + 0.5)
            rows.append(row)
        cols = jnp.concatenate(rows + [jnp.zeros((4, members), jnp.float32)], axis=0).T
        d = [
            jnp.broadcast_to(cols[:, c : c + 1], (members, members)) - tgt[c] for c in range(3)
        ]
        squared = d[0] * d[0] + d[1] * d[1] + d[2] * d[2]
        r = squared * lax.rsqrt(jnp.maximum(squared, 1e-30))
        t = 1.0 / (1.0 + 0.5 * r)
        poly = ERFCX[-1] * t + ERFCX[-2]
        for coefficient in ERFCX[-3::-1]:
            poly = poly * t + coefficient
        screened = jnp.exp(-squared) * (poly * t + (2.0 / math.sqrt(math.pi)) * r)
        inv = lax.rsqrt(squared + SOFTEN * SOFTEN)
        w = cols[:, 3:4] * screened * (inv * inv * inv)
        for c in range(3):
            total[c] = total[c] + jnp.sum(w * d[c], axis=0, keepdims=True)
    forces[job] = jnp.concatenate(total + [jnp.zeros((5, members), jnp.float32)], axis=0)


def kernel(
    zg,
    yg,
    leaf_cell,
    exports,
    tile_lists,
    fraction,
    masses,
    out,
    zt,
    recv,
    books,
    green,
    ee_hi,
    ee_lo,
    exact,
    short_tables,
    spectrum,
    q_hi,
    q_lo,
    msgs,
    back,
    forces,
    wz_hi,
    wz_lo,
    basis,
    lone_basis,
    planar,
    near_send,
    near_recv,
    sends,
    recvs,
):
    n_wide, n_narrow = lax.axis_size("wide"), lax.axis_size("narrow")
    ranks = n_wide * n_narrow
    leaves = leaf_cell.shape[1]
    slots = exports.shape[0]
    members = books.shape[3]
    nkz = G // zg
    nky = G // yg
    half_z = nkz // 2
    half = G // 2
    w, v = lax.axis_index("wide"), lax.axis_index("narrow")
    me = w * n_narrow + v
    my_z, my_y = lax.rem(me, zg), lax.div(me, zg)
    f32 = jnp.float32

    span = ranks // 2
    blocks = ranks // CHUNK
    cols = CHUNK * leaves
    levels = 2 if yg == 1 else 1
    low = nky // levels
    half_y = nky // 2
    strip = half_y // levels
    first_y = my_y * half_y

    barrier = pltpu.get_barrier_semaphore()

    def greet(at, column, to):
        pl.semaphore_signal(barrier, inc=1, device_id=to, device_id_type=pl.DeviceIdType.MESH)

    for far in (1, 0):
        each_peer(far, greet)

    leaf_row = iota((leaves, members), 0)
    lane = iota((1, members), 1)
    for c, extent in enumerate((PX, PY, PZ)):
        cell = jnp.zeros((leaves, members), f32)
        for n in range(leaves):
            cell = jnp.where(leaf_row == n, leaf_cell[c, n].astype(f32), cell)
        u = jnp.concatenate(
            [fraction[c : c + 1, n * members : (n + 1) * members] for n in range(leaves)], axis=0
        )
        books[0, c] = cell + (u * (extent - 1.0) + 0.5)
    books[0, 3] = jnp.concatenate(
        [masses[:, n * members : (n + 1) * members] for n in range(leaves)], axis=0
    )
    lists = jnp.zeros((leaves, members), f32)
    for n in range(leaves):
        both = jnp.where(
            lane < members // 2, tile_lists[0, n].astype(f32), tile_lists[1, n].astype(f32)
        )
        lists = jnp.where(leaf_row == n, both, lists)
    books[0, 4] = lists

    particles = leaves * members
    patch_row = iota((AB, particles), 0)
    planar_weights = None
    for c, extent, index in ((0, PX, patch_row // PY), (1, PY, patch_row % PY)):
        coordinate = 0.5 + fraction[c : c + 1, :] * (extent - 1.0)
        part = jnp.maximum(0.0, 1.0 - jnp.abs(coordinate - (index.astype(f32) + 0.5)))
        planar_weights = part if planar_weights is None else planar_weights * part
    planar[...] = planar_weights
    coordinate = 0.5 + fraction[2:3, :] * (PZ - 1.0)
    deep = jnp.maximum(
        0.0, 1.0 - jnp.abs(coordinate - (iota((PZ, particles), 0).astype(f32) + 0.5))
    )
    deep_hi, deep_lo = split(deep)
    wz_hi[...] = jnp.zeros_like(wz_hi)
    wz_lo[...] = jnp.zeros_like(wz_lo)
    for n in range(leaves):
        at = slice(n * members, (n + 1) * members)
        wz_hi[n * PZ : (n + 1) * PZ, at] = deep_hi[:, at]
        wz_lo[n * PZ : (n + 1) * PZ, at] = deep_lo[:, at]
    weighted = split(jnp.concatenate([planar_weights * masses[...]] * leaves, axis=0))
    width = leaves * PZ
    lone = leaves * AB
    patches = dot3((wz_hi[...], wz_lo[...]), weighted, ((1,), (1,)))
    same = iota((width, lone), 0) // PZ == iota((width, lone), 1) // AB
    patches = jnp.where(same, patches, 0.0)
    empty = jnp.zeros_like(patches)
    patches = split(
        jnp.concatenate(
            [
                jnp.concatenate([patches, empty], axis=1),
                jnp.concatenate([empty, patches], axis=1),
            ],
            axis=0,
        )
    )

    column = iota((1, width), 1)
    place = (column % PZ).astype(f32)
    note = jnp.zeros((1, 2 * lone), f32)
    for n in range(leaves):
        place = jnp.where(column // PZ == n, place + leaf_cell[2, n].astype(f32), place)
        for c in range(2):
            note = jnp.where(
                iota((1, 2 * lone), 1) // AB == c * leaves + n, leaf_cell[c, n].astype(f32), note
            )
    alternate = 1.0 - 2.0 * (place.astype(jnp.int32) & 1).astype(f32)
    row = iota((zg * SLOT, 1), 0)
    wave = row % half_z * zg + row // SLOT
    c, s = sincos(wave.astype(f32) * place)
    s = jnp.where(wave == 0, alternate, s)
    flat = dot3(split(jnp.concatenate([c, s], axis=1)), patches)
    zt[...] = jnp.where(row % SLOT == half_z, note, flat)

    pl.semaphore_wait(barrier, ranks - 1)

    for far in (1, 0):

        def send_out(at, column, to):
            group = lax.rem(at * n_narrow + column, zg)
            remote(
                zt.at[pl.ds(pl.multiple_of(group * SLOT, SLOT), half_z + 1), :],
                recv.at[pl.ds(pl.multiple_of(place_of(far, w, v) * SLOT, SLOT), half_z + 1), :],
                sends.at[far],
                recvs.at[far],
                to,
            ).start()

        each_peer(far, send_out)
    near = []
    for face, to in enumerate(
        (
            {"wide": lax.rem(w + n_wide - 1, n_wide), "narrow": v},
            {"wide": lax.rem(w + 1, n_wide), "narrow": v},
            {"wide": w, "narrow": lax.rem(v + n_narrow - 1, n_narrow)},
            {"wide": w, "narrow": lax.rem(v + 1, n_narrow)},
        )
    ):
        near.append(
            remote(books.at[0], books.at[face + 1], near_send.at[face], near_recv.at[face], to)
        )
    for copy in near:
        copy.start()

    recv[pl.ds(pl.multiple_of(place_of(0, w, v) * SLOT, SLOT), SLOT), :] = zt[
        pl.ds(pl.multiple_of(my_z * SLOT, SLOT), SLOT), :
    ]

    row = iota((half, 1), 0)
    wave = row
    c, s = sincos(wave.astype(f32) * place)
    tilt = slope(wave)
    psi = split(tilt * s) + split(-(tilt * c))
    s = jnp.where(wave == 0, alternate, s)
    for i, table in enumerate(split(c) + split(s)):
        for step in range(half_z):
            at = (2 * step + i // 2) * zg
            basis[i % 2, at : at + zg, :] = table[step * zg : (step + 1) * zg, :]
    for i, table in enumerate(psi):
        lone_basis[i] = table

    unit = 2.0 * math.pi / G
    wave_x, _ = real_mode(iota((1, G), 1), G)
    index_y = iota((nky, 1), 0)
    wave_y = first_y + index_y // (2 * strip) * strip + index_y % strip
    wave_y = jnp.where((wave_y == 0) & (index_y % (2 * strip) >= strip), half, wave_y)
    kx = wave_x.astype(f32) * unit
    ky = wave_y.astype(f32) * unit
    plane = kx * kx + ky * ky
    top = jnp.exp(-plane * (SCREEN * SCREEN)) * (share(wave_x) * share(wave_y))

    def fill_green(j, carry):
        wave_z = jnp.full((1, 1), lax.rem(j, half_z) * zg + my_z, jnp.int32)
        wave_z = jnp.where((wave_z == 0) & (j >= half_z), half, wave_z)
        kz = wave_z.astype(f32) * unit
        kz2 = kz * kz
        scale = jnp.exp(-kz2 * (SCREEN * SCREEN)) * share(wave_z) * (-4.0 * math.pi / G**3)
        total = plane + kz2
        green[j] = jnp.where(total > 0, top * scale / jnp.where(total > 0, total, 1.0), 0.0)
        return carry

    lax.fori_loop(0, nkz, fill_green, 0)

    def own(n, carry):
        pair_job(n, 0, n, leaf_cell, books, forces)
        return carry

    lax.fori_loop(0, leaves, own, 0)

    def received(far, at, buffer, rows):
        whole = buffer.at[pl.ds(0, (span - 1 + far) * rows), :]
        return remote(
            whole,
            whole,
            sends.at[at + far],
            recvs.at[at + far],
            {"wide": lax.rem(w + 1, n_wide), "narrow": v},
        )

    def gathered(block, j):
        turned = recv[pl.ds(block * CHUNK * SLOT + j, CHUNK, SLOT), :].T
        return [
            jnp.concatenate(
                [
                    turned[part * lone + n * AB : part * lone + (n + 1) * AB, :]
                    for n in range(leaves)
                ],
                axis=1,
            )
            for part in range(2)
        ]

    def tables(block):
        place_x, place_y = gathered(block, half_z)
        value, tilt = axis_tables(place_x[0:1, :], half, 0, PX)
        for a in range(PX):
            for kind, table in enumerate((value[a], tilt[a])):
                at = slice((kind * PX + a) * cols, (kind * PX + a + 1) * cols)
                for part in range(2):
                    hi, lo = split(table[part])
                    ee_hi[block, part * half : (part + 1) * half, at] = hi
                    ee_lo[block, part * half : (part + 1) * half, at] = lo
        value, tilt = axis_tables(place_y[0:1, :], half_y, first_y, PY)
        for b in range(PY):
            for kind, table in enumerate((value[b], tilt[b])):
                for level in range(levels):
                    for part in range(2):
                        at = (2 * level + part) * strip
                        rows = table[part][level * strip : (level + 1) * strip, :]
                        exact[block, kind * PY + b, at : at + strip, :] = rows
                        short_tables[block, kind * PY + b, at : at + strip, :] = rows.astype(
                            jnp.bfloat16
                        )

    def mixed(rows, block, table, first, last):
        halves = []
        for a in range(PX):
            m = None
            for b in range(PY):
                term = rows[a * PY + b : a * PY + b + 1, :] * table[block, b, first:last, :]
                m = term if m is None else m + term
            halves.append(m)
        return jnp.concatenate(halves, axis=1)

    nt = functools.partial(
        lax.dot_general,
        dimension_numbers=(((1,), (1,)), ((), ())),
        preferred_element_type=f32,
    )
    nn = functools.partial(jnp.dot, preferred_element_type=f32)

    def stacked(hi, lo, table_hi, table_lo, dot):
        if lo is None:
            return dot(hi, table_hi)
        rows, extra = hi.shape[0], lo.shape[0]
        both = dot(jnp.concatenate([hi, lo], axis=0), table_hi)
        first = both[0:extra] + (both[rows:] + dot(hi[0:extra], table_lo))
        return first if extra == rows else jnp.concatenate([first, both[extra:rows]], axis=0)

    def mix(block, j, edge):
        parts = gathered(block, j)
        pieces, lo = [], None
        if edge:
            hi, lo = split(
                jnp.concatenate([mixed(p, block, exact, 0, edge) for p in parts], axis=0)
            )
            pieces.append(hi)
        if edge < nky:
            pieces += [
                mixed(p.astype(jnp.bfloat16), block, short_tables, edge, nky) for p in parts
            ]
        return jnp.concatenate(pieces, axis=0), lo

    def forward(block, put):
        at = slice(0, PX * cols)
        ready = mix(block, 0, edge_of(0))
        for j in range(half_z):
            edge = edge_of(j)
            q = stacked(*ready, ee_hi[block, :, at], ee_lo[block, :, at], nt)
            if j + 1 < half_z:
                ready = mix(block, j + 1, edge_of(j + 1))
            for part in range(2):
                for first, last in ((0, edge), (edge, nky)):
                    if first < last:
                        count = last - first
                        start = 2 * first + part * count
                        put(part * half_z + j, first, last, q[start : start + count])

    def contracted(u, block, table, first, last):
        found = []
        count = last - first
        for kind, bank in ((1, 0), (0, 1), (0, 0)):
            for a in range(PX):
                at = (kind * PX + a) * cols
                column = u[:, at : at + cols]
                for b in range(PY):
                    term = column * table[block, bank * PY + b, first:last, :]
                    step = 32
                    total = term[0:step]
                    for i in range(step, count, step):
                        total = total + term[i : i + step]
                    found.append(jnp.sum(total.astype(f32), axis=0, keepdims=True))
        return jnp.concatenate(found, axis=0)

    def fields_of(block, j, edge):
        def rows(buffer, first, last):
            return [buffer[part * half_z + j, first:last] for part in range(2) if first < last]

        hi = jnp.concatenate(rows(q_hi, 0, edge) + rows(q_hi, edge, nky), axis=0)
        lo = jnp.concatenate(rows(q_lo, 0, edge), axis=0) if edge else None
        return stacked(hi, lo, ee_hi[block], ee_lo[block], nn)

    def finish(block, j, edge, u):
        count = nky - edge
        alone = []
        for part in range(2):
            field = 0.0
            if edge:
                field = contracted(u[part * edge : (part + 1) * edge], block, exact, 0, edge)
            if count:
                start = 2 * edge + part * count
                field += contracted(
                    u[start : start + count].astype(jnp.bfloat16), block, short_tables, edge, nky
                )
            pair = jnp.concatenate(
                [field[0 : 2 * AB, n * CHUNK : (n + 1) * CHUNK] for n in range(leaves)], axis=0
            )
            alone += [field[2 * AB :, n * CHUNK : (n + 1) * CHUNK] for n in range(leaves)]
            msgs[pl.ds(block * CHUNK * BACK + j * 3 + part, CHUNK, BACK), :] = pair.T
        at = block * CHUNK * BACK + j * 3 + 2
        msgs[pl.ds(at, CHUNK, BACK), :] = jnp.concatenate(alone, axis=0).T

    def inverse(block):
        ready = fields_of(block, 0, edge_of(0))
        for j in range(half_z):
            u = ready
            if j + 1 < half_z:
                ready = fields_of(block, j + 1, edge_of(j + 1))
            finish(block, j, edge_of(j), u)

    def edge_of(j):
        return low if j * zg < G // 4 else 0

    def begin(block):
        tables(block)

        def put(at, first, last, values):
            spectrum[at, first:last, :] = values

        forward(block, put)

    def go_on(block, carry):
        tables(block)

        def put(at, first, last, values):
            spectrum[at, first:last, :] += values

        forward(block, put)
        return carry

    def close(block):
        tables(block)

        def put(at, first, last, values):
            q = (spectrum[at, first:last, :] + values) * green[at, first:last, :]
            if first < edge_of(at % half_z):
                q_hi[at, first:last, :], q_lo[at, first:last, :] = split(q)
            else:
                q_hi[at, first:last, :] = q.astype(jnp.bfloat16)

        forward(block, put)

    received(0, 0, recv, half_z + 1).wait_recv()
    begin(0)
    lax.fori_loop(1, blocks // 2, go_on, 0)
    received(1, 0, recv, half_z + 1).wait_recv()
    lax.fori_loop(blocks // 2, blocks - 1, go_on, 0)
    close(blocks - 1)

    for far in (1, 0):

        def back_block(block, carry):
            inverse(block)
            return carry

        if blocks == 2:
            back_block(far, 0)
        else:
            lax.fori_loop(far * (blocks // 2), (far + 1) * (blocks // 2), back_block, 0)

        def send_back(at, column, to):
            place = pl.multiple_of(place_of(far, at, column) * BACK, BACK)
            remote(
                msgs.at[pl.ds(place, 3 * half_z), :],
                back.at[pl.ds(pl.multiple_of(me * BACK, BACK), 3 * half_z), :],
                sends.at[2 + far],
                recvs.at[2 + far],
                to,
            ).start()

        each_peer(far, send_back)
    back[pl.ds(pl.multiple_of(me * BACK, BACK), BACK), :] = msgs[
        pl.ds(pl.multiple_of(place_of(0, w, v) * BACK, BACK), BACK), :
    ]

    for copy in near:
        copy.wait_recv()

    def guest(j, carry):
        face = j // slots
        target = jnp.minimum(exports[j % slots, face], leaves - 1)
        pair_job(leaves + j, face + 1, target, leaf_cell, books, forces)
        return carry

    lax.fori_loop(0, 4 * slots, guest, 0)
    short = []
    for n in range(leaves):
        force = forces[n]
        for j in range(4 * slots):
            mine_too = jnp.where(exports[j % slots, j // slots] == n, 1.0, 0.0)
            force = force + forces[leaves + j] * mine_too
        short.append(force)
    short = jnp.concatenate(short, axis=1)

    for far in (0, 1):
        received(far, 2, back, 3 * half_z).wait_recv()

    def summed(j, part):
        total = back[pl.ds(j * 3 + part, zg, BACK), :]
        for h in range(1, yg):
            total = total + back[pl.ds(h * zg * BACK + j * 3 + part, zg, BACK), :]
        return total

    def own_part(table, start, rows):
        kept = jnp.where(column // PZ == 0, table[start : start + rows, :], 0.0)
        for n in range(1, leaves):
            at = start + n * rows
            kept = kept + jnp.where(column // PZ == n, table[at : at + rows, :], 0.0)
        return kept

    pairs = jnp.concatenate([summed(i // 2, i % 2) for i in range(nkz)], axis=0)
    along = dot3(split(pairs), (basis[0], basis[1]), ((0,), (0,)))
    lones = split(jnp.concatenate([summed(i, 2) for i in range(half_z)], axis=0))
    deep = None
    for part in range(2):
        rows = dot3(lones, (lone_basis[2 * part], lone_basis[2 * part + 1]), ((0,), (0,)))
        rows = own_part(rows, part * lone, AB)
        deep = rows if deep is None else deep + rows
    sampled = [own_part(along, 0, PZ), deep]
    sampled = jnp.concatenate(sampled, axis=0)
    got = dot3(split(sampled), (wz_hi[...], wz_lo[...]))
    for c in range(3):
        out[c : c + 1, :] = (
            jnp.sum(got[c * AB : (c + 1) * AB, :] * planar[...], axis=0, keepdims=True)
            + short[c : c + 1, :]
        )
    for copy in near:
        copy.wait_send()
    for far in range(2):
        received(far, 0, recv, half_z + 1).wait_send()
        received(far, 2, back, 3 * half_z).wait_send()


def local(fraction, masses, leaf_cell, exports, tile_lists):
    leaves = leaf_cell.shape[1]
    members = masses.shape[0] // leaves
    slots = exports.shape[1]
    ranks = lax.axis_size("wide") * lax.axis_size("narrow")
    f32, bf16 = jnp.float32, jnp.bfloat16
    zg = min(ranks, G // 8)
    yg = ranks // zg
    nkz, nky = G // zg, G // yg
    cols = CHUNK * leaves
    width = leaves * PZ
    blocks = ranks // CHUNK
    return pl.pallas_call(
        functools.partial(kernel, zg, yg),
        out_shape=pltpu.VMEM((3, leaves * members), f32),
        in_specs=[SMEM, SMEM, SMEM, VMEM, VMEM],
        out_specs=VMEM,
        scratch_shapes=[
            pltpu.VMEM((zg * SLOT, width), f32),
            pltpu.VMEM((ranks * SLOT, width), f32),
            pltpu.VMEM((5, 5, leaves, members), f32),
            pltpu.VMEM((nkz, nky, G), f32),
            pltpu.VMEM((blocks, G, 2 * PX * cols), bf16),
            pltpu.VMEM((blocks, G, 2 * PX * cols), bf16),
            pltpu.VMEM((blocks, 2 * PY, nky, cols), f32),
            pltpu.VMEM((blocks, 2 * PY, nky, cols), bf16),
            pltpu.VMEM((nkz, nky, G), f32),
            pltpu.VMEM((nkz, nky, G), bf16),
            pltpu.VMEM((nkz, nky, G), bf16),
            pltpu.VMEM((ranks * BACK, width), f32),
            pltpu.VMEM((ranks * BACK, width), f32),
            pltpu.VMEM((leaves + 4 * slots, 8, members), f32),
            pltpu.VMEM((width, leaves * members), bf16),
            pltpu.VMEM((width, leaves * members), bf16),
            pltpu.VMEM((2, G, width), bf16),
            pltpu.VMEM((4, G // 2, width), bf16),
            pltpu.VMEM((AB, leaves * members), f32),
            pltpu.SemaphoreType.DMA((4,)),
            pltpu.SemaphoreType.DMA((4,)),
            pltpu.SemaphoreType.DMA((4,)),
            pltpu.SemaphoreType.DMA((4,)),
        ],
        compiler_params=pltpu.CompilerParams(
            collective_id=0, has_side_effects=True, vmem_limit_bytes=56 * 2**20
        ),
        name="treepm",
    )(leaf_cell, exports.T, tile_lists, fraction, masses.reshape(1, -1))


def solution(mesh):
    placed = (
        P(None, ("wide", "narrow")),
        P(("wide", "narrow")),
        P(None, ("wide", "narrow")),
        P(None, ("wide", "narrow")),
        P(None, ("wide", "narrow")),
    )
    return jax.shard_map(
        local, mesh=mesh, in_specs=placed, out_specs=P(None, ("wide", "narrow")), check_vma=False
    )
```

```python
import functools
import math

import jax
import jax.numpy as jnp
from jax import lax
from jax.experimental import pallas as pl
from jax.experimental.pallas import tpu as pltpu
from jax.sharding import PartitionSpec as P

G = 256
PX = 2
PY = 4
PZ = 16
AB = PX * PY
SLOT = 8
BACK = 16
CHUNK = 16
SCREEN = 0.5
SOFTEN = 0.5
ERFCX = (
    0.2820947416810428,
    0.28210427504184366,
    0.24651391069954823,
    0.18039116519942175,
    0.058372405908860704,
    0.0792320361696661,
    -0.1983246779625943,
    0.030722780905291756,
    0.06437369661731697,
    -0.025480486181070308,
)
VMEM = pl.BlockSpec(memory_space=pltpu.VMEM)
ANY = pl.BlockSpec(memory_space=pl.ANY)


def iota(shape, dim):
    return lax.broadcasted_iota(jnp.int32, shape, dim)


def sincos(count):
    quarters = count * (4.0 / G)
    near = jnp.floor(quarters + 0.5)
    z = (quarters - near) * (math.pi / 2)
    q = near.astype(jnp.int32)
    zz = z * z
    c = 1.0 + zz * (-0.5 + zz * (1.0 / 24 + zz * (-1.0 / 720 + zz * (1.0 / 40320))))
    s = z * (1.0 + zz * (-1.0 / 6 + zz * (1.0 / 120 + zz * (-1.0 / 5040))))
    swap = (q & 1) == 1
    cosine = jnp.where(swap, s, c)
    sine = jnp.where(swap, c, s)
    cosine = jnp.where(((q + 1) & 2) == 2, -cosine, cosine)
    sine = jnp.where((q & 2) == 2, -sine, sine)
    return cosine, sine


def split(x):
    hi = x.astype(jnp.bfloat16)
    return hi, (x - hi.astype(jnp.float32)).astype(jnp.bfloat16)


def dot3(left, right, dims=((1,), (0,))):
    dims = (dims, ((), ()))
    dot = functools.partial(
        lax.dot_general, dimension_numbers=dims, preferred_element_type=jnp.float32
    )
    return dot(left[0], right[0]) + (dot(left[0], right[1]) + dot(left[1], right[0]))


def slope(wave):
    w = wave.astype(jnp.float32)
    return (8.0 * sincos(w)[1] - sincos(2.0 * w)[1]) * (1.0 / 6.0)


def real_mode(index, count):
    half = count // 2
    wave = index // count * half + index % half
    second = (index % count) // half
    top = (second == 1) & (wave == 0)
    sine = (second == 1) & (wave > 0)
    return jnp.where(top, G // 2, wave), sine


def share(wave):
    return jnp.where(wave % (G // 2) == 0, 1.0, 2.0)


def each_peer(far, visit):
    n_wide, n_narrow = lax.axis_size("wide"), lax.axis_size("narrow")
    w, v = lax.axis_index("wide"), lax.axis_index("narrow")
    span = n_narrow // 2
    start = lax.rem(lax.div(v, span) + far, 2) * span
    columns = [start + lax.rem(lax.rem(v, span) + b, span) for b in range(span)]

    def row(at, first):
        for column in columns[first:]:
            visit(at, column, {"wide": at, "narrow": column})

    row(w, 1 - far)
    if n_wide <= 8:
        for a in range(1, n_wide):
            row(lax.rem(w + a, n_wide), 0)
    else:

        def step(a, carry):
            row(lax.rem(w + a, n_wide), 0)
            return carry

        lax.fori_loop(1, n_wide, step, 0)


def place_of(far, w, v):
    n_wide, n_narrow = lax.axis_size("wide"), lax.axis_size("narrow")
    span = n_narrow // 2
    return (far * n_wide + w) * span + lax.rem(v, span)


def remote(src, dst, send, recv, to):
    return pltpu.make_async_remote_copy(
        src_ref=src,
        dst_ref=dst,
        send_sem=send,
        recv_sem=recv,
        device_id=to,
        device_id_type=pl.DeviceIdType.MESH,
    )


def axis_tables(position, waves, first, steps):
    rows = waves
    row = iota((rows, 1), 0)
    wave = first + row
    c, s = sincos(wave.astype(jnp.float32) * position)
    turn_c, turn_s = sincos(wave.astype(jnp.float32))
    tilt = slope(wave)
    alternate = 1.0 - 2.0 * (position.astype(jnp.int32) & 1).astype(jnp.float32)
    top = wave == 0
    values, slopes = [], []
    for b in range(steps):
        if b:
            c, s = c * turn_c - s * turn_s, s * turn_c + c * turn_s
            alternate = -alternate
        values.append((c, jnp.where(top, alternate, s)))
        slopes.append((tilt * s, -(tilt * c)))
    return values, slopes


def pair_job(job, rank, target, leaf_cell, books, forces):
    members = books.shape[3]
    leaves = books.shape[2]
    leaf = iota((leaves, members), 0).astype(jnp.float32)
    lane = iota((1, members), 1)
    tgt = [books[0, c, pl.ds(target, 1), :] for c in range(3)]
    origin = [leaf_cell[c, target].astype(jnp.float32) for c in range(3)]
    lists = books[rank, 4, pl.ds(target, 1), :]
    swapped = pltpu.roll(lists, members // 2, 1)
    total = [0.0, 0.0, 0.0]
    for k in range(2):
        wanted = jnp.where((lane < members // 2) == (k == 0), lists, swapped)
        mine = leaf == wanted
        rows = []
        for c in range(4):
            row = jnp.sum(jnp.where(mine, books[rank, c], 0.0), axis=0, keepdims=True)
            if c < 3:
                row = row - G * jnp.floor((row - origin[c]) * (1.0 / G) + 0.5)
            rows.append(row)
        cols = jnp.concatenate(rows + [jnp.zeros((4, members), jnp.float32)], axis=0).T
        d = [
            jnp.broadcast_to(cols[:, c : c + 1], (members, members)) - tgt[c] for c in range(3)
        ]
        squared = d[0] * d[0] + d[1] * d[1] + d[2] * d[2]
        r = squared * lax.rsqrt(jnp.maximum(squared, 1e-30))
        t = 1.0 / (1.0 + 0.5 * r)
        poly = ERFCX[-1] * t + ERFCX[-2]
        for coefficient in ERFCX[-3::-1]:
            poly = poly * t + coefficient
        screened = jnp.exp(-squared) * (poly * t + (2.0 / math.sqrt(math.pi)) * r)
        inv = lax.rsqrt(squared + SOFTEN * SOFTEN)
        w = cols[:, 3:4] * screened * (inv * inv * inv)
        for c in range(3):
            total[c] = total[c] + jnp.sum(w * d[c], axis=0, keepdims=True)
    forces[job] = jnp.concatenate(total + [jnp.zeros((5, members), jnp.float32)], axis=0)


def kernel(
    zg,
    yg,
    leaf_cell_in,
    exports_in,
    tile_lists_in,
    fraction_in,
    masses_in,
    out,
    leaf_cell,
    exports,
    tile_lists,
    fraction,
    masses,
    loads,
    zt,
    recv,
    books,
    green,
    ee_hi,
    ee_lo,
    exact,
    short_tables,
    spectrum,
    q_hi,
    q_lo,
    msgs,
    back,
    forces,
    wz_hi,
    wz_lo,
    basis,
    lone_basis,
    planar,
    near_send,
    near_recv,
    sends,
    recvs,
):
    n_wide, n_narrow = lax.axis_size("wide"), lax.axis_size("narrow")
    ranks = n_wide * n_narrow
    leaves = leaf_cell.shape[1]
    slots = exports.shape[0]
    members = books.shape[3]
    nkz = G // zg
    nky = G // yg
    half_z = nkz // 2
    half = G // 2
    w, v = lax.axis_index("wide"), lax.axis_index("narrow")
    me = w * n_narrow + v
    my_z, my_y = lax.rem(me, zg), lax.div(me, zg)
    f32 = jnp.float32

    span = ranks // 2
    blocks = ranks // CHUNK
    cols = CHUNK * leaves
    levels = 2 if yg == 1 else 1
    low = nky // levels
    half_y = nky // 2
    strip = half_y // levels
    first_y = my_y * half_y

    barrier = pltpu.get_barrier_semaphore()

    def greet(at, column, to):
        pl.semaphore_signal(barrier, inc=1, device_id=to, device_id_type=pl.DeviceIdType.MESH)

    for far in (1, 0):
        each_peer(far, greet)

    arguments = [
        pltpu.make_async_copy(src, dst, loads.at[i])
        for i, (src, dst) in enumerate(
            (
                (leaf_cell_in, leaf_cell),
                (exports_in, exports),
                (tile_lists_in, tile_lists),
                (fraction_in, fraction),
                (masses_in, masses),
            )
        )
    ]
    for copy in arguments:
        copy.start()
    for copy in arguments:
        copy.wait()

    leaf_row = iota((leaves, members), 0)
    lane = iota((1, members), 1)
    for c, extent in enumerate((PX, PY, PZ)):
        cell = jnp.zeros((leaves, members), f32)
        for n in range(leaves):
            cell = jnp.where(leaf_row == n, leaf_cell[c, n].astype(f32), cell)
        u = jnp.concatenate(
            [fraction[c : c + 1, n * members : (n + 1) * members] for n in range(leaves)], axis=0
        )
        books[0, c] = cell + (u * (extent - 1.0) + 0.5)
    books[0, 3] = jnp.concatenate(
        [masses[:, n * members : (n + 1) * members] for n in range(leaves)], axis=0
    )
    lists = jnp.zeros((leaves, members), f32)
    for n in range(leaves):
        both = jnp.where(
            lane < members // 2, tile_lists[0, n].astype(f32), tile_lists[1, n].astype(f32)
        )
        lists = jnp.where(leaf_row == n, both, lists)
    books[0, 4] = lists

    particles = leaves * members
    patch_row = iota((AB, particles), 0)
    planar_weights = None
    for c, extent, index in ((0, PX, patch_row // PY), (1, PY, patch_row % PY)):
        coordinate = 0.5 + fraction[c : c + 1, :] * (extent - 1.0)
        part = jnp.maximum(0.0, 1.0 - jnp.abs(coordinate - (index.astype(f32) + 0.5)))
        planar_weights = part if planar_weights is None else planar_weights * part
    planar[...] = planar_weights
    coordinate = 0.5 + fraction[2:3, :] * (PZ - 1.0)
    deep = jnp.maximum(
        0.0, 1.0 - jnp.abs(coordinate - (iota((PZ, particles), 0).astype(f32) + 0.5))
    )
    deep_hi, deep_lo = split(deep)
    wz_hi[...] = jnp.zeros_like(wz_hi)
    wz_lo[...] = jnp.zeros_like(wz_lo)
    for n in range(leaves):
        at = slice(n * members, (n + 1) * members)
        wz_hi[n * PZ : (n + 1) * PZ, at] = deep_hi[:, at]
        wz_lo[n * PZ : (n + 1) * PZ, at] = deep_lo[:, at]
    weighted = split(jnp.concatenate([planar_weights * masses[...]] * leaves, axis=0))
    width = leaves * PZ
    lone = leaves * AB
    patches = dot3((wz_hi[...], wz_lo[...]), weighted, ((1,), (1,)))
    same = iota((width, lone), 0) // PZ == iota((width, lone), 1) // AB
    patches = jnp.where(same, patches, 0.0)
    empty = jnp.zeros_like(patches)
    patches = split(
        jnp.concatenate(
            [
                jnp.concatenate([patches, empty], axis=1),
                jnp.concatenate([empty, patches], axis=1),
            ],
            axis=0,
        )
    )

    column = iota((1, width), 1)
    place = (column % PZ).astype(f32)
    note = jnp.zeros((1, 2 * lone), f32)
    for n in range(leaves):
        place = jnp.where(column // PZ == n, place + leaf_cell[2, n].astype(f32), place)
        for c in range(2):
            note = jnp.where(
                iota((1, 2 * lone), 1) // AB == c * leaves + n, leaf_cell[c, n].astype(f32), note
            )
    alternate = 1.0 - 2.0 * (place.astype(jnp.int32) & 1).astype(f32)
    row = iota((zg * SLOT, 1), 0)
    wave = row % half_z * zg + row // SLOT
    c, s = sincos(wave.astype(f32) * place)
    s = jnp.where(wave == 0, alternate, s)
    flat = dot3(split(jnp.concatenate([c, s], axis=1)), patches)
    zt[...] = jnp.where(row % SLOT == half_z, note, flat)

    def own(n, carry):
        pair_job(n, 0, n, leaf_cell, books, forces)
        return carry

    sooner = leaves * (n_narrow - 1 - v) // (n_narrow - 1)
    lax.fori_loop(0, sooner, own, 0)
    pl.semaphore_wait(barrier, ranks - 1)

    for far in (1, 0):

        def send_out(at, column, to):
            group = lax.rem(at * n_narrow + column, zg)
            remote(
                zt.at[pl.ds(pl.multiple_of(group * SLOT, SLOT), half_z + 1), :],
                recv.at[pl.ds(pl.multiple_of(place_of(far, w, v) * SLOT, SLOT), half_z + 1), :],
                sends.at[far],
                recvs.at[far],
                to,
            ).start()

        each_peer(far, send_out)
    near = []
    for face, to in enumerate(
        (
            {"wide": lax.rem(w + n_wide - 1, n_wide), "narrow": v},
            {"wide": lax.rem(w + 1, n_wide), "narrow": v},
            {"wide": w, "narrow": lax.rem(v + n_narrow - 1, n_narrow)},
            {"wide": w, "narrow": lax.rem(v + 1, n_narrow)},
        )
    ):
        near.append(
            remote(books.at[0], books.at[face + 1], near_send.at[face], near_recv.at[face], to)
        )
    for copy in near:
        copy.start()

    recv[pl.ds(pl.multiple_of(place_of(0, w, v) * SLOT, SLOT), SLOT), :] = zt[
        pl.ds(pl.multiple_of(my_z * SLOT, SLOT), SLOT), :
    ]

    row = iota((half, 1), 0)
    wave = row
    c, s = sincos(wave.astype(f32) * place)
    tilt = slope(wave)
    psi = split(tilt * s) + split(-(tilt * c))
    s = jnp.where(wave == 0, alternate, s)
    for i, table in enumerate(split(c) + split(s)):
        for step in range(half_z):
            at = (2 * step + i // 2) * zg
            basis[i % 2, at : at + zg, :] = table[step * zg : (step + 1) * zg, :]
    for i, table in enumerate(psi):
        lone_basis[i] = table

    unit = 2.0 * math.pi / G
    wave_x, _ = real_mode(iota((1, G), 1), G)
    index_y = iota((nky, 1), 0)
    wave_y = first_y + index_y // (2 * strip) * strip + index_y % strip
    wave_y = jnp.where((wave_y == 0) & (index_y % (2 * strip) >= strip), half, wave_y)
    kx = wave_x.astype(f32) * unit
    ky = wave_y.astype(f32) * unit
    plane = kx * kx + ky * ky
    top = jnp.exp(-plane * (SCREEN * SCREEN)) * (share(wave_x) * share(wave_y))

    def fill_green(j, carry):
        wave_z = jnp.full((1, 1), lax.rem(j, half_z) * zg + my_z, jnp.int32)
        wave_z = jnp.where((wave_z == 0) & (j >= half_z), half, wave_z)
        kz = wave_z.astype(f32) * unit
        kz2 = kz * kz
        scale = jnp.exp(-kz2 * (SCREEN * SCREEN)) * share(wave_z) * (-4.0 * math.pi / G**3)
        total = plane + kz2
        green[j] = jnp.where(total > 0, top * scale / jnp.where(total > 0, total, 1.0), 0.0)
        return carry

    lax.fori_loop(0, half_z + 1, fill_green, 0)

    lax.fori_loop(sooner, leaves, own, 0)

    def received(far, at, buffer, rows):
        whole = buffer.at[pl.ds(0, (span - 1 + far) * rows), :]
        return remote(
            whole,
            whole,
            sends.at[at + far],
            recvs.at[at + far],
            {"wide": lax.rem(w + 1, n_wide), "narrow": v},
        )

    def gathered(block, j):
        turned = recv[pl.ds(block * CHUNK * SLOT + j, CHUNK, SLOT), :].T
        return [
            jnp.concatenate(
                [
                    turned[part * lone + n * AB : part * lone + (n + 1) * AB, :]
                    for n in range(leaves)
                ],
                axis=1,
            )
            for part in range(2)
        ]

    def tables(block):
        place_x, place_y = gathered(block, half_z)
        value, tilt = axis_tables(place_x[0:1, :], half, 0, PX)
        for a in range(PX):
            for kind, table in enumerate((value[a], tilt[a])):
                at = slice((kind * PX + a) * cols, (kind * PX + a + 1) * cols)
                for part in range(2):
                    hi, lo = split(table[part])
                    ee_hi[block, part * half : (part + 1) * half, at] = hi
                    ee_lo[block, part * half : (part + 1) * half, at] = lo
        value, tilt = axis_tables(place_y[0:1, :], half_y, first_y, PY)
        for b in range(PY):
            for kind, table in enumerate((value[b], tilt[b])):
                for level in range(levels):
                    for part in range(2):
                        at = (2 * level + part) * strip
                        rows = table[part][level * strip : (level + 1) * strip, :]
                        exact[block, kind * PY + b, at : at + strip, :] = rows
                        short_tables[block, kind * PY + b, at : at + strip, :] = rows.astype(
                            jnp.bfloat16
                        )

    def mixed(rows, block, table, first, last):
        halves = []
        for a in range(PX):
            m = None
            for b in range(PY):
                term = rows[a * PY + b : a * PY + b + 1, :] * table[block, b, first:last, :]
                m = term if m is None else m + term
            halves.append(m)
        return jnp.concatenate(halves, axis=1)

    nt = functools.partial(
        lax.dot_general,
        dimension_numbers=(((1,), (1,)), ((), ())),
        preferred_element_type=f32,
    )
    nn = functools.partial(jnp.dot, preferred_element_type=f32)

    def stacked(hi, lo, table_hi, table_lo, dot):
        if lo is None:
            return dot(hi, table_hi)
        rows, extra = hi.shape[0], lo.shape[0]
        both = dot(jnp.concatenate([hi, lo], axis=0), table_hi)
        first = both[0:extra] + (both[rows:] + dot(hi[0:extra], table_lo))
        return first if extra == rows else jnp.concatenate([first, both[extra:rows]], axis=0)

    def mix(block, j, edge):
        parts = gathered(block, j)
        pieces, lo = [], None
        if edge:
            hi, lo = split(
                jnp.concatenate([mixed(p, block, exact, 0, edge) for p in parts], axis=0)
            )
            pieces.append(hi)
        if edge < nky:
            pieces += [
                mixed(p.astype(jnp.bfloat16), block, short_tables, edge, nky) for p in parts
            ]
        return jnp.concatenate(pieces, axis=0), lo

    def forward(block, put):
        at = slice(0, PX * cols)
        ready = mix(block, 0, edge_of(0))
        for j in range(half_z):
            edge = edge_of(j)
            q = stacked(*ready, ee_hi[block, :, at], ee_lo[block, :, at], nt)
            if j + 1 < half_z:
                ready = mix(block, j + 1, edge_of(j + 1))
            for part in range(2):
                for first, last in ((0, edge), (edge, nky)):
                    if first < last:
                        count = last - first
                        start = 2 * first + part * count
                        put(part * half_z + j, first, last, q[start : start + count])

    def contracted(u, block, table, first, last):
        found = []
        count = last - first
        for kind, bank in ((1, 0), (0, 1), (0, 0)):
            for a in range(PX):
                at = (kind * PX + a) * cols
                column = u[:, at : at + cols]
                for b in range(PY):
                    term = column * table[block, bank * PY + b, first:last, :]
                    step = 16
                    total = term[0:step]
                    for i in range(step, count, step):
                        total = total + term[i : i + step]
                    found.append(jnp.sum(total.astype(f32), axis=0, keepdims=True))
        return jnp.concatenate(found, axis=0)

    def fields_of(block, j, edge):
        def rows(buffer, first, last):
            return [buffer[part * half_z + j, first:last] for part in range(2) if first < last]

        hi = jnp.concatenate(rows(q_hi, 0, edge) + rows(q_hi, edge, nky), axis=0)
        lo = jnp.concatenate(rows(q_lo, 0, edge), axis=0) if edge else None
        return stacked(hi, lo, ee_hi[block], ee_lo[block], nn)

    def finish(block, j, edge, u):
        count = nky - edge
        alone = []
        for part in range(2):
            field = 0.0
            if edge:
                field = contracted(u[part * edge : (part + 1) * edge], block, exact, 0, edge)
            if count:
                start = 2 * edge + part * count
                field += contracted(
                    u[start : start + count].astype(jnp.bfloat16), block, short_tables, edge, nky
                )
            pair = jnp.concatenate(
                [field[0 : 2 * AB, n * CHUNK : (n + 1) * CHUNK] for n in range(leaves)], axis=0
            )
            alone += [field[2 * AB :, n * CHUNK : (n + 1) * CHUNK] for n in range(leaves)]
            msgs[pl.ds(block * CHUNK * BACK + j * 3 + part, CHUNK, BACK), :] = pair.T
        at = block * CHUNK * BACK + j * 3 + 2
        msgs[pl.ds(at, CHUNK, BACK), :] = jnp.concatenate(alone, axis=0).T

    def inverse(block):
        ready = fields_of(block, 0, edge_of(0))
        for j in range(half_z):
            u = ready
            if j + 1 < half_z:
                ready = fields_of(block, j + 1, edge_of(j + 1))
            finish(block, j, edge_of(j), u)

    def edge_of(j):
        return low if j * zg < G // 4 else 0

    def begin(block):
        tables(block)

        def put(at, first, last, values):
            spectrum[at, first:last, :] = values

        forward(block, put)

    def go_on(block, carry):
        tables(block)

        def put(at, first, last, values):
            spectrum[at, first:last, :] += values

        forward(block, put)
        return carry

    def close(block):
        tables(block)

        def put(at, first, last, values):
            q = (spectrum[at, first:last, :] + values) * green[min(at, half_z) if at % half_z == 0 else at % half_z, first:last, :]
            if first < edge_of(at % half_z):
                q_hi[at, first:last, :], q_lo[at, first:last, :] = split(q)
            else:
                q_hi[at, first:last, :] = q.astype(jnp.bfloat16)

        forward(block, put)

    received(0, 0, recv, half_z + 1).wait_recv()
    begin(0)
    lax.fori_loop(1, blocks // 2, go_on, 0)
    received(1, 0, recv, half_z + 1).wait_recv()
    lax.fori_loop(blocks // 2, blocks - 1, go_on, 0)
    close(blocks - 1)

    for far in (1, 0):

        def back_block(block, carry):
            inverse(block)
            return carry

        if blocks == 2:
            back_block(far, 0)
        else:
            lax.fori_loop(far * (blocks // 2), (far + 1) * (blocks // 2), back_block, 0)

        def send_back(at, column, to):
            place = pl.multiple_of(place_of(far, at, column) * BACK, BACK)
            remote(
                msgs.at[pl.ds(place, 3 * half_z), :],
                back.at[pl.ds(pl.multiple_of(me * BACK, BACK), 3 * half_z), :],
                sends.at[2 + far],
                recvs.at[2 + far],
                to,
            ).start()

        each_peer(far, send_back)
    back[pl.ds(pl.multiple_of(me * BACK, BACK), BACK), :] = msgs[
        pl.ds(pl.multiple_of(place_of(0, w, v) * BACK, BACK), BACK), :
    ]

    for copy in near:
        copy.wait_recv()

    def guest(j, carry):
        face = j // slots
        target = jnp.minimum(exports[j % slots, face], leaves - 1)
        pair_job(leaves + j, face + 1, target, leaf_cell, books, forces)
        return carry

    lax.fori_loop(0, 4 * slots, guest, 0)
    short = []
    for n in range(leaves):
        force = forces[n]
        for j in range(4 * slots):
            mine_too = jnp.where(exports[j % slots, j // slots] == n, 1.0, 0.0)
            force = force + forces[leaves + j] * mine_too
        short.append(force)
    short = jnp.concatenate(short, axis=1)

    for far in (0, 1):
        received(far, 2, back, 3 * half_z).wait_recv()

    def summed(j, part):
        total = back[pl.ds(j * 3 + part, zg, BACK), :]
        for h in range(1, yg):
            total = total + back[pl.ds(h * zg * BACK + j * 3 + part, zg, BACK), :]
        return total

    def own_part(table, start, rows):
        kept = jnp.where(column // PZ == 0, table[start : start + rows, :], 0.0)
        for n in range(1, leaves):
            at = start + n * rows
            kept = kept + jnp.where(column // PZ == n, table[at : at + rows, :], 0.0)
        return kept

    pairs = jnp.concatenate([summed(i // 2, i % 2) for i in range(nkz)], axis=0)
    along = dot3(split(pairs), (basis[0], basis[1]), ((0,), (0,)))
    lones = split(jnp.concatenate([summed(i, 2) for i in range(half_z)], axis=0))
    deep = None
    for part in range(2):
        rows = dot3(lones, (lone_basis[2 * part], lone_basis[2 * part + 1]), ((0,), (0,)))
        rows = own_part(rows, part * lone, AB)
        deep = rows if deep is None else deep + rows
    sampled = [own_part(along, 0, PZ), deep]
    sampled = jnp.concatenate(sampled, axis=0)
    got = dot3(split(sampled), (wz_hi[...], wz_lo[...]))
    for c in range(3):
        out[c : c + 1, :] = (
            jnp.sum(got[c * AB : (c + 1) * AB, :] * planar[...], axis=0, keepdims=True)
            + short[c : c + 1, :]
        )
    for copy in near:
        copy.wait_send()
    for far in range(2):
        received(far, 0, recv, half_z + 1).wait_send()
        received(far, 2, back, 3 * half_z).wait_send()


def local(fraction, masses, leaf_cell, exports, tile_lists):
    leaves = leaf_cell.shape[1]
    members = masses.shape[0] // leaves
    slots = exports.shape[1]
    ranks = lax.axis_size("wide") * lax.axis_size("narrow")
    f32, bf16 = jnp.float32, jnp.bfloat16
    zg = min(ranks, G // 8)
    yg = ranks // zg
    nkz, nky = G // zg, G // yg
    cols = CHUNK * leaves
    width = leaves * PZ
    blocks = ranks // CHUNK
    return pl.pallas_call(
        functools.partial(kernel, zg, yg),
        out_shape=pltpu.VMEM((3, leaves * members), f32),
        in_specs=[ANY] * 5,
        out_specs=VMEM,
        scratch_shapes=[
            pltpu.SMEM(leaf_cell.shape, jnp.int32),
            pltpu.SMEM((slots, exports.shape[0]), jnp.int32),
            pltpu.SMEM(tile_lists.shape, jnp.int32),
            pltpu.VMEM(fraction.shape, f32),
            pltpu.VMEM((1, leaves * members), f32),
            pltpu.SemaphoreType.DMA((5,)),
            pltpu.VMEM((zg * SLOT, width), f32),
            pltpu.VMEM((ranks * SLOT, width), f32),
            pltpu.VMEM((5, 5, leaves, members), f32),
            pltpu.VMEM((nkz // 2 + 1, nky, G), f32),
            pltpu.VMEM((blocks, G, 2 * PX * cols), bf16),
            pltpu.VMEM((blocks, G, 2 * PX * cols), bf16),
            pltpu.VMEM((blocks, 2 * PY, nky, cols), f32),
            pltpu.VMEM((blocks, 2 * PY, nky, cols), bf16),
            pltpu.VMEM((nkz, nky, G), f32),
            pltpu.VMEM((nkz, nky, G), bf16),
            pltpu.VMEM((nkz, nky, G), bf16),
            pltpu.VMEM((ranks * BACK, width), f32),
            pltpu.VMEM((ranks * BACK, width), f32),
            pltpu.VMEM((leaves + 4 * slots, 8, members), f32),
            pltpu.VMEM((width, leaves * members), bf16),
            pltpu.VMEM((width, leaves * members), bf16),
            pltpu.VMEM((2, G, width), bf16),
            pltpu.VMEM((4, G // 2, width), bf16),
            pltpu.VMEM((AB, leaves * members), f32),
            pltpu.SemaphoreType.DMA((4,)),
            pltpu.SemaphoreType.DMA((4,)),
            pltpu.SemaphoreType.DMA((4,)),
            pltpu.SemaphoreType.DMA((4,)),
        ],
        compiler_params=pltpu.CompilerParams(
            collective_id=0, has_side_effects=True, vmem_limit_bytes=56 * 2**20
        ),
        name="treepm",
    )(leaf_cell, exports.T, tile_lists, fraction, masses.reshape(1, -1))


def solution(mesh):
    placed = (
        P(None, ("wide", "narrow")),
        P(("wide", "narrow")),
        P(None, ("wide", "narrow")),
        P(None, ("wide", "narrow")),
        P(None, ("wide", "narrow")),
    )
    return jax.shard_map(
        local, mesh=mesh, in_specs=placed, out_specs=P(None, ("wide", "narrow")), check_vma=False
    )
```

```python
import functools
import math

import jax
import jax.numpy as jnp
from jax import lax
from jax.experimental import pallas as pl
from jax.experimental.pallas import tpu as pltpu
from jax.sharding import PartitionSpec as P

G = 256
PX = 2
PY = 4
PZ = 16
AB = PX * PY
SLOT = 8
BACK = 16
CHUNK = 16
SCREEN = 0.5
SOFTEN = 0.5
ERFCX = (
    0.2820947416810428,
    0.28210427504184366,
    0.24651391069954823,
    0.18039116519942175,
    0.058372405908860704,
    0.0792320361696661,
    -0.1983246779625943,
    0.030722780905291756,
    0.06437369661731697,
    -0.025480486181070308,
)
VMEM = pl.BlockSpec(memory_space=pltpu.VMEM)
ANY = pl.BlockSpec(memory_space=pl.ANY)


def iota(shape, dim):
    return lax.broadcasted_iota(jnp.int32, shape, dim)


def sincos(count):
    quarters = count * (4.0 / G)
    near = jnp.floor(quarters + 0.5)
    z = (quarters - near) * (math.pi / 2)
    q = near.astype(jnp.int32)
    zz = z * z
    c = 1.0 + zz * (-0.5 + zz * (1.0 / 24 + zz * (-1.0 / 720 + zz * (1.0 / 40320))))
    s = z * (1.0 + zz * (-1.0 / 6 + zz * (1.0 / 120 + zz * (-1.0 / 5040))))
    swap = (q & 1) == 1
    cosine = jnp.where(swap, s, c)
    sine = jnp.where(swap, c, s)
    cosine = jnp.where(((q + 1) & 2) == 2, -cosine, cosine)
    sine = jnp.where((q & 2) == 2, -sine, sine)
    return cosine, sine


def split(x):
    hi = x.astype(jnp.bfloat16)
    return hi, (x - hi.astype(jnp.float32)).astype(jnp.bfloat16)


def dot3(left, right, dims=((1,), (0,))):
    dims = (dims, ((), ()))
    dot = functools.partial(
        lax.dot_general, dimension_numbers=dims, preferred_element_type=jnp.float32
    )
    return dot(left[0], right[0]) + (dot(left[0], right[1]) + dot(left[1], right[0]))


def slope(wave):
    w = wave.astype(jnp.float32)
    return (8.0 * sincos(w)[1] - sincos(2.0 * w)[1]) * (1.0 / 6.0)


def real_mode(index, count):
    half = count // 2
    wave = index // count * half + index % half
    second = (index % count) // half
    top = (second == 1) & (wave == 0)
    sine = (second == 1) & (wave > 0)
    return jnp.where(top, G // 2, wave), sine


def share(wave):
    return jnp.where(wave % (G // 2) == 0, 1.0, 2.0)


def each_peer(far, visit):
    n_wide, n_narrow = lax.axis_size("wide"), lax.axis_size("narrow")
    w, v = lax.axis_index("wide"), lax.axis_index("narrow")
    span = n_narrow // 2
    start = lax.rem(lax.div(v, span) + far, 2) * span
    columns = [start + lax.rem(lax.rem(v, span) + b, span) for b in range(span)]

    def row(at, first):
        for column in columns[first:]:
            visit(at, column, {"wide": at, "narrow": column})

    row(w, 1 - far)
    if n_wide <= 8:
        for a in range(1, n_wide):
            row(lax.rem(w + a, n_wide), 0)
    else:

        def step(a, carry):
            row(lax.rem(w + a, n_wide), 0)
            return carry

        lax.fori_loop(1, n_wide, step, 0)


def place_of(far, w, v):
    n_wide, n_narrow = lax.axis_size("wide"), lax.axis_size("narrow")
    span = n_narrow // 2
    return (far * n_wide + w) * span + lax.rem(v, span)


def remote(src, dst, send, recv, to):
    return pltpu.make_async_remote_copy(
        src_ref=src,
        dst_ref=dst,
        send_sem=send,
        recv_sem=recv,
        device_id=to,
        device_id_type=pl.DeviceIdType.MESH,
    )


def axis_tables(position, waves, first, steps):
    rows = waves
    row = iota((rows, 1), 0)
    wave = first + row
    c, s = sincos(wave.astype(jnp.float32) * position)
    turn_c, turn_s = sincos(wave.astype(jnp.float32))
    tilt = slope(wave)
    alternate = 1.0 - 2.0 * (position.astype(jnp.int32) & 1).astype(jnp.float32)
    top = wave == 0
    values, slopes = [], []
    for b in range(steps):
        if b:
            c, s = c * turn_c - s * turn_s, s * turn_c + c * turn_s
            alternate = -alternate
        values.append((c, jnp.where(top, alternate, s)))
        slopes.append((tilt * s, -(tilt * c)))
    return values, slopes


def pair_job(job, rank, target, leaf_cell, books, forces):
    members = books.shape[3]
    leaves = books.shape[2]
    leaf = iota((leaves, members), 0).astype(jnp.float32)
    lane = iota((1, members), 1)
    tgt = [books[0, c, pl.ds(target, 1), :] for c in range(3)]
    origin = [leaf_cell[c, target].astype(jnp.float32) for c in range(3)]
    lists = books[rank, 4, pl.ds(target, 1), :]
    swapped = pltpu.roll(lists, members // 2, 1)
    total = [0.0, 0.0, 0.0]
    for k in range(2):
        wanted = jnp.where((lane < members // 2) == (k == 0), lists, swapped)
        mine = leaf == wanted
        rows = []
        for c in range(4):
            row = jnp.sum(jnp.where(mine, books[rank, c], 0.0), axis=0, keepdims=True)
            if c < 3:
                row = row - G * jnp.floor((row - origin[c]) * (1.0 / G) + 0.5)
            rows.append(row)
        cols = jnp.concatenate(rows + [jnp.zeros((4, members), jnp.float32)], axis=0).T
        d = [
            jnp.broadcast_to(cols[:, c : c + 1], (members, members)) - tgt[c] for c in range(3)
        ]
        squared = d[0] * d[0] + d[1] * d[1] + d[2] * d[2]
        r = squared * lax.rsqrt(jnp.maximum(squared, 1e-30))
        t = 1.0 / (1.0 + 0.5 * r)
        poly = ERFCX[-1] * t + ERFCX[-2]
        for coefficient in ERFCX[-3::-1]:
            poly = poly * t + coefficient
        screened = jnp.exp(-squared) * (poly * t + (2.0 / math.sqrt(math.pi)) * r)
        inv = lax.rsqrt(squared + SOFTEN * SOFTEN)
        w = cols[:, 3:4] * screened * (inv * inv * inv)
        for c in range(3):
            total[c] = total[c] + jnp.sum(w * d[c], axis=0, keepdims=True)
    forces[job] = jnp.concatenate(total + [jnp.zeros((5, members), jnp.float32)], axis=0)


def kernel(
    zg,
    yg,
    leaf_cell_in,
    exports_in,
    tile_lists_in,
    fraction_in,
    masses_in,
    out,
    leaf_cell,
    exports,
    tile_lists,
    fraction,
    masses,
    loads,
    zt,
    recv,
    books,
    green,
    ee_hi,
    ee_lo,
    exact,
    short_tables,
    spectrum,
    q_hi,
    q_lo,
    msgs,
    back,
    forces,
    wz_hi,
    wz_lo,
    basis,
    lone_basis,
    planar,
    near_send,
    near_recv,
    sends,
    recvs,
):
    n_wide, n_narrow = lax.axis_size("wide"), lax.axis_size("narrow")
    ranks = n_wide * n_narrow
    leaves = leaf_cell.shape[1]
    slots = exports.shape[0]
    members = books.shape[3]
    nkz = G // zg
    nky = G // yg
    half_z = nkz // 2
    half = G // 2
    w, v = lax.axis_index("wide"), lax.axis_index("narrow")
    me = w * n_narrow + v
    my_z, my_y = lax.rem(me, zg), lax.div(me, zg)
    f32 = jnp.float32

    span = ranks // 2
    blocks = ranks // CHUNK
    cols = CHUNK * leaves
    levels = 2 if yg == 1 else 1
    low = nky // levels
    half_y = nky // 2
    strip = half_y // levels
    first_y = my_y * half_y

    half_j = half_z // 2

    def row_of(j, part):
        return j // half_j * SLOT + j % half_j * 3 + part

    barrier = pltpu.get_barrier_semaphore()

    def greet(at, column, to):
        pl.semaphore_signal(barrier, inc=1, device_id=to, device_id_type=pl.DeviceIdType.MESH)

    for far in (1, 0):
        each_peer(far, greet)

    arguments = [
        pltpu.make_async_copy(src, dst, loads.at[i])
        for i, (src, dst) in enumerate(
            (
                (leaf_cell_in, leaf_cell),
                (exports_in, exports),
                (tile_lists_in, tile_lists),
                (fraction_in, fraction),
                (masses_in, masses),
            )
        )
    ]
    for copy in arguments:
        copy.start()
    for copy in arguments:
        copy.wait()

    leaf_row = iota((leaves, members), 0)
    lane = iota((1, members), 1)
    for c, extent in enumerate((PX, PY, PZ)):
        cell = jnp.zeros((leaves, members), f32)
        for n in range(leaves):
            cell = jnp.where(leaf_row == n, leaf_cell[c, n].astype(f32), cell)
        u = jnp.concatenate(
            [fraction[c : c + 1, n * members : (n + 1) * members] for n in range(leaves)], axis=0
        )
        books[0, c] = cell + (u * (extent - 1.0) + 0.5)
    books[0, 3] = jnp.concatenate(
        [masses[:, n * members : (n + 1) * members] for n in range(leaves)], axis=0
    )
    lists = jnp.zeros((leaves, members), f32)
    for n in range(leaves):
        both = jnp.where(
            lane < members // 2, tile_lists[0, n].astype(f32), tile_lists[1, n].astype(f32)
        )
        lists = jnp.where(leaf_row == n, both, lists)
    books[0, 4] = lists

    particles = leaves * members
    patch_row = iota((AB, particles), 0)
    planar_weights = None
    for c, extent, index in ((0, PX, patch_row // PY), (1, PY, patch_row % PY)):
        coordinate = 0.5 + fraction[c : c + 1, :] * (extent - 1.0)
        part = jnp.maximum(0.0, 1.0 - jnp.abs(coordinate - (index.astype(f32) + 0.5)))
        planar_weights = part if planar_weights is None else planar_weights * part
    planar[...] = planar_weights
    coordinate = 0.5 + fraction[2:3, :] * (PZ - 1.0)
    deep = jnp.maximum(
        0.0, 1.0 - jnp.abs(coordinate - (iota((PZ, particles), 0).astype(f32) + 0.5))
    )
    deep_hi, deep_lo = split(deep)
    wz_hi[...] = jnp.zeros_like(wz_hi)
    wz_lo[...] = jnp.zeros_like(wz_lo)
    for n in range(leaves):
        at = slice(n * members, (n + 1) * members)
        wz_hi[n * PZ : (n + 1) * PZ, at] = deep_hi[:, at]
        wz_lo[n * PZ : (n + 1) * PZ, at] = deep_lo[:, at]
    weighted = split(jnp.concatenate([planar_weights * masses[...]] * leaves, axis=0))
    width = leaves * PZ
    lone = leaves * AB
    patches = dot3((wz_hi[...], wz_lo[...]), weighted, ((1,), (1,)))
    same = iota((width, lone), 0) // PZ == iota((width, lone), 1) // AB
    patches = jnp.where(same, patches, 0.0)
    empty = jnp.zeros_like(patches)
    patches = split(
        jnp.concatenate(
            [
                jnp.concatenate([patches, empty], axis=1),
                jnp.concatenate([empty, patches], axis=1),
            ],
            axis=0,
        )
    )

    column = iota((1, width), 1)
    place = (column % PZ).astype(f32)
    note = jnp.zeros((1, 2 * lone), f32)
    for n in range(leaves):
        place = jnp.where(column // PZ == n, place + leaf_cell[2, n].astype(f32), place)
        for c in range(2):
            note = jnp.where(
                iota((1, 2 * lone), 1) // AB == c * leaves + n, leaf_cell[c, n].astype(f32), note
            )
    alternate = 1.0 - 2.0 * (place.astype(jnp.int32) & 1).astype(f32)
    row = iota((zg * SLOT, 1), 0)
    wave = row % half_z * zg + row // SLOT
    c, s = sincos(wave.astype(f32) * place)
    s = jnp.where(wave == 0, alternate, s)
    flat = dot3(split(jnp.concatenate([c, s], axis=1)), patches)
    zt[...] = jnp.where(row % SLOT == half_z, note, flat)

    def own(n, carry):
        pair_job(n, 0, n, leaf_cell, books, forces)
        return carry

    sooner = leaves // 4
    lax.fori_loop(0, sooner, own, 0)
    pl.semaphore_wait(barrier, ranks - 1)

    for far in (1, 0):

        def send_out(at, column, to):
            group = lax.rem(at * n_narrow + column, zg)
            remote(
                zt.at[pl.ds(pl.multiple_of(group * SLOT, SLOT), half_z + 1), :],
                recv.at[pl.ds(pl.multiple_of(place_of(far, w, v) * SLOT, SLOT), half_z + 1), :],
                sends.at[far],
                recvs.at[far],
                to,
            ).start()

        each_peer(far, send_out)
    near = []
    for face, to in enumerate(
        (
            {"wide": lax.rem(w + n_wide - 1, n_wide), "narrow": v},
            {"wide": lax.rem(w + 1, n_wide), "narrow": v},
            {"wide": w, "narrow": lax.rem(v + n_narrow - 1, n_narrow)},
            {"wide": w, "narrow": lax.rem(v + 1, n_narrow)},
        )
    ):
        near.append(
            remote(books.at[0], books.at[face + 1], near_send.at[face], near_recv.at[face], to)
        )
    for copy in near:
        copy.start()

    recv[pl.ds(pl.multiple_of(place_of(0, w, v) * SLOT, SLOT), SLOT), :] = zt[
        pl.ds(pl.multiple_of(my_z * SLOT, SLOT), SLOT), :
    ]

    row = iota((half, 1), 0)
    wave = row
    c, s = sincos(wave.astype(f32) * place)
    tilt = slope(wave)
    psi = split(tilt * s) + split(-(tilt * c))
    s = jnp.where(wave == 0, alternate, s)
    for i, table in enumerate(split(c) + split(s)):
        for step in range(half_z):
            at = (2 * step + i // 2) * zg
            basis[i % 2, at : at + zg, :] = table[step * zg : (step + 1) * zg, :]
    for i, table in enumerate(psi):
        lone_basis[i] = table

    unit = 2.0 * math.pi / G
    wave_x, _ = real_mode(iota((1, G), 1), G)
    index_y = iota((nky, 1), 0)
    wave_y = first_y + index_y // (2 * strip) * strip + index_y % strip
    wave_y = jnp.where((wave_y == 0) & (index_y % (2 * strip) >= strip), half, wave_y)
    kx = wave_x.astype(f32) * unit
    ky = wave_y.astype(f32) * unit
    plane = kx * kx + ky * ky
    top = jnp.exp(-plane * (SCREEN * SCREEN)) * (share(wave_x) * share(wave_y))

    def fill_green(j, carry):
        wave_z = jnp.full((1, 1), lax.rem(j, half_z) * zg + my_z, jnp.int32)
        wave_z = jnp.where((wave_z == 0) & (j >= half_z), half, wave_z)
        kz = wave_z.astype(f32) * unit
        kz2 = kz * kz
        scale = jnp.exp(-kz2 * (SCREEN * SCREEN)) * share(wave_z) * (-4.0 * math.pi / G**3)
        total = plane + kz2
        green[j] = jnp.where(total > 0, top * scale / jnp.where(total > 0, total, 1.0), 0.0)
        return carry

    lax.fori_loop(0, half_z + 1, fill_green, 0)

    lax.fori_loop(sooner, leaves, own, 0)

    def received(far, at, buffer, rows):
        whole = buffer.at[pl.ds(0, (span - 1 + far) * rows), :]
        return remote(
            whole,
            whole,
            sends.at[at + far],
            recvs.at[at + far],
            {"wide": lax.rem(w + 1, n_wide), "narrow": v},
        )

    def gathered(block, j):
        turned = recv[pl.ds(block * CHUNK * SLOT + j, CHUNK, SLOT), :].T
        return [
            jnp.concatenate(
                [
                    turned[part * lone + n * AB : part * lone + (n + 1) * AB, :]
                    for n in range(leaves)
                ],
                axis=1,
            )
            for part in range(2)
        ]

    def tables(block):
        place_x, place_y = gathered(block, half_z)
        value, tilt = axis_tables(place_x[0:1, :], half, 0, PX)
        for a in range(PX):
            for kind, table in enumerate((value[a], tilt[a])):
                at = slice((kind * PX + a) * cols, (kind * PX + a + 1) * cols)
                for part in range(2):
                    hi, lo = split(table[part])
                    ee_hi[block, part * half : (part + 1) * half, at] = hi
                    ee_lo[block, part * half : (part + 1) * half, at] = lo
        value, tilt = axis_tables(place_y[0:1, :], half_y, first_y, PY)
        for b in range(PY):
            for kind, table in enumerate((value[b], tilt[b])):
                for level in range(levels):
                    for part in range(2):
                        at = (2 * level + part) * strip
                        rows = table[part][level * strip : (level + 1) * strip, :]
                        exact[block, kind * PY + b, at : at + strip, :] = rows
                        short_tables[block, kind * PY + b, at : at + strip, :] = rows.astype(
                            jnp.bfloat16
                        )

    def mixed(rows, block, table, first, last):
        halves = []
        for a in range(PX):
            m = None
            for b in range(PY):
                term = rows[a * PY + b : a * PY + b + 1, :] * table[block, b, first:last, :]
                m = term if m is None else m + term
            halves.append(m)
        return jnp.concatenate(halves, axis=1)

    nt = functools.partial(
        lax.dot_general,
        dimension_numbers=(((1,), (1,)), ((), ())),
        preferred_element_type=f32,
    )
    nn = functools.partial(jnp.dot, preferred_element_type=f32)

    def stacked(hi, lo, table_hi, table_lo, dot):
        if lo is None:
            return dot(hi, table_hi)
        rows, extra = hi.shape[0], lo.shape[0]
        both = dot(jnp.concatenate([hi, lo], axis=0), table_hi)
        first = both[0:extra] + (both[rows:] + dot(hi[0:extra], table_lo))
        return first if extra == rows else jnp.concatenate([first, both[extra:rows]], axis=0)

    def mix(block, j, edge):
        parts = gathered(block, j)
        pieces, lo = [], None
        if edge:
            hi, lo = split(
                jnp.concatenate([mixed(p, block, exact, 0, edge) for p in parts], axis=0)
            )
            pieces.append(hi)
        if edge < nky:
            pieces += [
                mixed(p.astype(jnp.bfloat16), block, short_tables, edge, nky) for p in parts
            ]
        return jnp.concatenate(pieces, axis=0), lo

    def forward(block, put):
        at = slice(0, PX * cols)
        ready = mix(block, 0, edge_of(0))
        for j in range(half_z):
            edge = edge_of(j)
            q = stacked(*ready, ee_hi[block, :, at], ee_lo[block, :, at], nt)
            if j + 1 < half_z:
                ready = mix(block, j + 1, edge_of(j + 1))
            for part in range(2):
                for first, last in ((0, edge), (edge, nky)):
                    if first < last:
                        count = last - first
                        start = 2 * first + part * count
                        put(part * half_z + j, first, last, q[start : start + count])

    def contracted(u, block, table, first, last):
        found = []
        count = last - first
        for kind, bank in ((1, 0), (0, 1), (0, 0)):
            for a in range(PX):
                at = (kind * PX + a) * cols
                column = u[:, at : at + cols]
                for b in range(PY):
                    term = column * table[block, bank * PY + b, first:last, :]
                    step = 16
                    total = term[0:step]
                    for i in range(step, count, step):
                        total = total + term[i : i + step]
                    found.append(jnp.sum(total.astype(f32), axis=0, keepdims=True))
        return jnp.concatenate(found, axis=0)

    def fields_of(block, j, edge):
        def rows(buffer, first, last):
            return [buffer[part * half_z + j, first:last] for part in range(2) if first < last]

        hi = jnp.concatenate(rows(q_hi, 0, edge) + rows(q_hi, edge, nky), axis=0)
        lo = jnp.concatenate(rows(q_lo, 0, edge), axis=0) if edge else None
        return stacked(hi, lo, ee_hi[block], ee_lo[block], nn)

    def finish(block, j, edge, u):
        count = nky - edge
        alone = []
        for part in range(2):
            field = 0.0
            if edge:
                field = contracted(u[part * edge : (part + 1) * edge], block, exact, 0, edge)
            if count:
                start = 2 * edge + part * count
                field += contracted(
                    u[start : start + count].astype(jnp.bfloat16), block, short_tables, edge, nky
                )
            pair = jnp.concatenate(
                [field[0 : 2 * AB, n * CHUNK : (n + 1) * CHUNK] for n in range(leaves)], axis=0
            )
            alone += [field[2 * AB :, n * CHUNK : (n + 1) * CHUNK] for n in range(leaves)]
            msgs[pl.ds(block * CHUNK * BACK + row_of(j, part), CHUNK, BACK), :] = pair.T
        at = block * CHUNK * BACK + row_of(j, 2)
        msgs[pl.ds(at, CHUNK, BACK), :] = jnp.concatenate(alone, axis=0).T

    def send_back(far, stage):
        def send(at, column, to):
            place = pl.multiple_of(place_of(far, at, column) * BACK + stage * SLOT, SLOT)
            landing = pl.multiple_of(me * BACK + stage * SLOT, SLOT)
            remote(
                msgs.at[pl.ds(place, 3 * half_j), :],
                back.at[pl.ds(landing, 3 * half_j), :],
                sends.at[2 + 2 * stage + far],
                recvs.at[2 + 2 * stage + far],
                to,
            ).start()

        each_peer(far, send)

    def inverse(block, sent=None):
        order = list(reversed(range(half_z)))
        ready = fields_of(block, order[0], edge_of(order[0]))
        for i, j in enumerate(order):
            u = ready
            if i + 1 < half_z:
                ready = fields_of(block, order[i + 1], edge_of(order[i + 1]))
            finish(block, j, edge_of(j), u)
            if sent is not None and j % half_j == 0:
                send_back(sent, j // half_j)

    def edge_of(j):
        return low if j * zg < G // 4 else 0

    def begin(block):
        tables(block)

        def put(at, first, last, values):
            spectrum[at, first:last, :] = values

        forward(block, put)

    def go_on(block, carry):
        tables(block)

        def put(at, first, last, values):
            spectrum[at, first:last, :] += values

        forward(block, put)
        return carry

    def close(block):
        tables(block)

        def put(at, first, last, values):
            q = (spectrum[at, first:last, :] + values) * green[min(at, half_z) if at % half_z == 0 else at % half_z, first:last, :]
            if first < edge_of(at % half_z):
                q_hi[at, first:last, :], q_lo[at, first:last, :] = split(q)
            else:
                q_hi[at, first:last, :] = q.astype(jnp.bfloat16)

        forward(block, put)

    received(0, 0, recv, half_z + 1).wait_recv()
    begin(0)
    lax.fori_loop(1, blocks // 2, go_on, 0)
    received(1, 0, recv, half_z + 1).wait_recv()
    lax.fori_loop(blocks // 2, blocks - 1, go_on, 0)
    close(blocks - 1)

    for far in (1, 0):
        if blocks == 2:
            inverse(far, far)
        else:

            def back_block(block, carry):
                inverse(block)
                return carry

            lax.fori_loop(far * (blocks // 2), (far + 1) * (blocks // 2), back_block, 0)
            for stage in range(2):
                send_back(far, stage)
    back[pl.ds(pl.multiple_of(me * BACK, BACK), BACK), :] = msgs[
        pl.ds(pl.multiple_of(place_of(0, w, v) * BACK, BACK), BACK), :
    ]

    for copy in near:
        copy.wait_recv()

    def guest(j, carry):
        face = j // slots
        target = jnp.minimum(exports[j % slots, face], leaves - 1)
        pair_job(leaves + j, face + 1, target, leaf_cell, books, forces)
        return carry

    lax.fori_loop(0, 4 * slots, guest, 0)
    short = []
    for n in range(leaves):
        force = forces[n]
        for j in range(4 * slots):
            mine_too = jnp.where(exports[j % slots, j // slots] == n, 1.0, 0.0)
            force = force + forces[leaves + j] * mine_too
        short.append(force)
    short = jnp.concatenate(short, axis=1)

    for stage in range(2):
        for far in (0, 1):
            received(far, 2 + 2 * stage, back, 3 * half_j).wait_recv()

    def summed(j, part):
        total = back[pl.ds(row_of(j, part), zg, BACK), :]
        for h in range(1, yg):
            total = total + back[pl.ds(h * zg * BACK + row_of(j, part), zg, BACK), :]
        return total

    def own_part(table, start, rows):
        kept = jnp.where(column // PZ == 0, table[start : start + rows, :], 0.0)
        for n in range(1, leaves):
            at = start + n * rows
            kept = kept + jnp.where(column // PZ == n, table[at : at + rows, :], 0.0)
        return kept

    pairs = jnp.concatenate([summed(i // 2, i % 2) for i in range(nkz)], axis=0)
    along = dot3(split(pairs), (basis[0], basis[1]), ((0,), (0,)))
    lones = split(jnp.concatenate([summed(i, 2) for i in range(half_z)], axis=0))
    deep = None
    for part in range(2):
        rows = dot3(lones, (lone_basis[2 * part], lone_basis[2 * part + 1]), ((0,), (0,)))
        rows = own_part(rows, part * lone, AB)
        deep = rows if deep is None else deep + rows
    sampled = [own_part(along, 0, PZ), deep]
    sampled = jnp.concatenate(sampled, axis=0)
    got = dot3(split(sampled), (wz_hi[...], wz_lo[...]))
    for c in range(3):
        out[c : c + 1, :] = (
            jnp.sum(got[c * AB : (c + 1) * AB, :] * planar[...], axis=0, keepdims=True)
            + short[c : c + 1, :]
        )
    for copy in near:
        copy.wait_send()
    for far in range(2):
        received(far, 0, recv, half_z + 1).wait_send()
        for stage in range(2):
            received(far, 2 + 2 * stage, back, 3 * half_j).wait_send()


def local(fraction, masses, leaf_cell, exports, tile_lists):
    leaves = leaf_cell.shape[1]
    members = masses.shape[0] // leaves
    slots = exports.shape[1]
    ranks = lax.axis_size("wide") * lax.axis_size("narrow")
    f32, bf16 = jnp.float32, jnp.bfloat16
    zg = min(ranks, G // 8)
    yg = ranks // zg
    nkz, nky = G // zg, G // yg
    cols = CHUNK * leaves
    width = leaves * PZ
    blocks = ranks // CHUNK
    return pl.pallas_call(
        functools.partial(kernel, zg, yg),
        out_shape=pltpu.VMEM((3, leaves * members), f32),
        in_specs=[ANY] * 5,
        out_specs=VMEM,
        scratch_shapes=[
            pltpu.SMEM(leaf_cell.shape, jnp.int32),
            pltpu.SMEM((slots, exports.shape[0]), jnp.int32),
            pltpu.SMEM(tile_lists.shape, jnp.int32),
            pltpu.VMEM(fraction.shape, f32),
            pltpu.VMEM((1, leaves * members), f32),
            pltpu.SemaphoreType.DMA((5,)),
            pltpu.VMEM((zg * SLOT, width), f32),
            pltpu.VMEM((ranks * SLOT, width), f32),
            pltpu.VMEM((5, 5, leaves, members), f32),
            pltpu.VMEM((nkz // 2 + 1, nky, G), f32),
            pltpu.VMEM((blocks, G, 2 * PX * cols), bf16),
            pltpu.VMEM((blocks, G, 2 * PX * cols), bf16),
            pltpu.VMEM((blocks, 2 * PY, nky, cols), f32),
            pltpu.VMEM((blocks, 2 * PY, nky, cols), bf16),
            pltpu.VMEM((nkz, nky, G), f32),
            pltpu.VMEM((nkz, nky, G), bf16),
            pltpu.VMEM((nkz, nky, G), bf16),
            pltpu.VMEM((ranks * BACK, width), f32),
            pltpu.VMEM((ranks * BACK, width), f32),
            pltpu.VMEM((leaves + 4 * slots, 8, members), f32),
            pltpu.VMEM((width, leaves * members), bf16),
            pltpu.VMEM((width, leaves * members), bf16),
            pltpu.VMEM((2, G, width), bf16),
            pltpu.VMEM((4, G // 2, width), bf16),
            pltpu.VMEM((AB, leaves * members), f32),
            pltpu.SemaphoreType.DMA((4,)),
            pltpu.SemaphoreType.DMA((4,)),
            pltpu.SemaphoreType.DMA((6,)),
            pltpu.SemaphoreType.DMA((6,)),
        ],
        compiler_params=pltpu.CompilerParams(
            collective_id=0, has_side_effects=True, vmem_limit_bytes=56 * 2**20
        ),
        name="treepm",
    )(leaf_cell, exports.T, tile_lists, fraction, masses.reshape(1, -1))


def solution(mesh):
    placed = (
        P(None, ("wide", "narrow")),
        P(("wide", "narrow")),
        P(None, ("wide", "narrow")),
        P(None, ("wide", "narrow")),
        P(None, ("wide", "narrow")),
    )
    return jax.shard_map(
        local, mesh=mesh, in_specs=placed, out_specs=P(None, ("wide", "narrow")), check_vma=False
    )
```

```python
import functools
import math

import jax
import jax.numpy as jnp
from jax import lax
from jax.experimental import pallas as pl
from jax.experimental.pallas import tpu as pltpu
from jax.sharding import PartitionSpec as P

G = 256
PX = 2
PY = 4
PZ = 16
AB = PX * PY
SLOT = 8
BACK = 16
CHUNK = 16
SCREEN = 0.5
SOFTEN = 0.5
ERFCX = (
    0.2820947416810428,
    0.28210427504184366,
    0.24651391069954823,
    0.18039116519942175,
    0.058372405908860704,
    0.0792320361696661,
    -0.1983246779625943,
    0.030722780905291756,
    0.06437369661731697,
    -0.025480486181070308,
)
VMEM = pl.BlockSpec(memory_space=pltpu.VMEM)
ANY = pl.BlockSpec(memory_space=pl.ANY)


def iota(shape, dim):
    return lax.broadcasted_iota(jnp.int32, shape, dim)


def sincos(count):
    quarters = count * (4.0 / G)
    near = jnp.floor(quarters + 0.5)
    z = (quarters - near) * (math.pi / 2)
    q = near.astype(jnp.int32)
    zz = z * z
    c = 1.0 + zz * (-0.5 + zz * (1.0 / 24 + zz * (-1.0 / 720 + zz * (1.0 / 40320))))
    s = z * (1.0 + zz * (-1.0 / 6 + zz * (1.0 / 120 + zz * (-1.0 / 5040))))
    swap = (q & 1) == 1
    cosine = jnp.where(swap, s, c)
    sine = jnp.where(swap, c, s)
    cosine = jnp.where(((q + 1) & 2) == 2, -cosine, cosine)
    sine = jnp.where((q & 2) == 2, -sine, sine)
    return cosine, sine


def split(x):
    hi = x.astype(jnp.bfloat16)
    return hi, (x - hi.astype(jnp.float32)).astype(jnp.bfloat16)


def dot3(left, right, dims=((1,), (0,))):
    dims = (dims, ((), ()))
    dot = functools.partial(
        lax.dot_general, dimension_numbers=dims, preferred_element_type=jnp.float32
    )
    return dot(left[0], right[0]) + (dot(left[0], right[1]) + dot(left[1], right[0]))


def slope(wave):
    w = wave.astype(jnp.float32)
    return (8.0 * sincos(w)[1] - sincos(2.0 * w)[1]) * (1.0 / 6.0)


def real_mode(index, count):
    half = count // 2
    wave = index // count * half + index % half
    second = (index % count) // half
    top = (second == 1) & (wave == 0)
    sine = (second == 1) & (wave > 0)
    return jnp.where(top, G // 2, wave), sine


def share(wave):
    return jnp.where(wave % (G // 2) == 0, 1.0, 2.0)


def each_peer(far, visit):
    n_wide, n_narrow = lax.axis_size("wide"), lax.axis_size("narrow")
    w, v = lax.axis_index("wide"), lax.axis_index("narrow")
    span = n_narrow // 2
    start = lax.rem(lax.div(v, span) + far, 2) * span
    columns = [start + lax.rem(lax.rem(v, span) + b, span) for b in range(span)]

    def row(at, first):
        for column in columns[first:]:
            visit(at, column, {"wide": at, "narrow": column})

    row(w, 1 - far)
    if n_wide <= 8:
        for a in range(1, n_wide):
            row(lax.rem(w + a, n_wide), 0)
    else:

        def step(a, carry):
            row(lax.rem(w + a, n_wide), 0)
            return carry

        lax.fori_loop(1, n_wide, step, 0)


def place_of(far, w, v):
    n_wide, n_narrow = lax.axis_size("wide"), lax.axis_size("narrow")
    span = n_narrow // 2
    return (far * n_wide + w) * span + lax.rem(v, span)


def remote(src, dst, send, recv, to):
    return pltpu.make_async_remote_copy(
        src_ref=src,
        dst_ref=dst,
        send_sem=send,
        recv_sem=recv,
        device_id=to,
        device_id_type=pl.DeviceIdType.MESH,
    )


def axis_tables(position, waves, first, steps):
    rows = waves
    row = iota((rows, 1), 0)
    wave = first + row
    c, s = sincos(wave.astype(jnp.float32) * position)
    turn_c, turn_s = sincos(wave.astype(jnp.float32))
    tilt = slope(wave)
    alternate = 1.0 - 2.0 * (position.astype(jnp.int32) & 1).astype(jnp.float32)
    top = wave == 0
    values, slopes = [], []
    for b in range(steps):
        if b:
            c, s = c * turn_c - s * turn_s, s * turn_c + c * turn_s
            alternate = -alternate
        values.append((c, jnp.where(top, alternate, s)))
        slopes.append((tilt * s, -(tilt * c)))
    return values, slopes


def pair_job(job, rank, target, leaf_cell, books, forces):
    members = books.shape[3]
    leaves = books.shape[2]
    leaf = iota((leaves, members), 0).astype(jnp.float32)
    lane = iota((1, members), 1)
    tgt = [books[0, c, pl.ds(target, 1), :] for c in range(3)]
    origin = [leaf_cell[c, target].astype(jnp.float32) for c in range(3)]
    lists = books[rank, 4, pl.ds(target, 1), :]
    swapped = pltpu.roll(lists, members // 2, 1)
    total = [0.0, 0.0, 0.0]
    for k in range(2):
        wanted = jnp.where((lane < members // 2) == (k == 0), lists, swapped)
        mine = leaf == wanted
        rows = []
        for c in range(4):
            row = jnp.sum(jnp.where(mine, books[rank, c], 0.0), axis=0, keepdims=True)
            if c < 3:
                row = row - G * jnp.floor((row - origin[c]) * (1.0 / G) + 0.5)
            rows.append(row)
        cols = jnp.concatenate(rows + [jnp.zeros((4, members), jnp.float32)], axis=0).T
        d = [
            jnp.broadcast_to(cols[:, c : c + 1], (members, members)) - tgt[c] for c in range(3)
        ]
        squared = d[0] * d[0] + d[1] * d[1] + d[2] * d[2]
        r = squared * lax.rsqrt(jnp.maximum(squared, 1e-30))
        t = 1.0 / (1.0 + 0.5 * r)
        poly = ERFCX[-1] * t + ERFCX[-2]
        for coefficient in ERFCX[-3::-1]:
            poly = poly * t + coefficient
        screened = jnp.exp(-squared) * (poly * t + (2.0 / math.sqrt(math.pi)) * r)
        inv = lax.rsqrt(squared + SOFTEN * SOFTEN)
        w = cols[:, 3:4] * screened * (inv * inv * inv)
        for c in range(3):
            total[c] = total[c] + jnp.sum(w * d[c], axis=0, keepdims=True)
    forces[job] = jnp.concatenate(total + [jnp.zeros((5, members), jnp.float32)], axis=0)


def kernel(
    zg,
    yg,
    leaf_cell_in,
    exports_in,
    tile_lists_in,
    fraction_in,
    masses_in,
    out,
    leaf_cell,
    exports,
    tile_lists,
    fraction,
    masses,
    loads,
    zt,
    recv,
    books,
    green,
    ee_hi,
    ee_lo,
    exact,
    short_tables,
    spectrum,
    q_hi,
    q_lo,
    msgs,
    back,
    forces,
    wz_hi,
    wz_lo,
    basis,
    lone_basis,
    planar,
    near_send,
    near_recv,
    sends,
    recvs,
):
    n_wide, n_narrow = lax.axis_size("wide"), lax.axis_size("narrow")
    ranks = n_wide * n_narrow
    leaves = leaf_cell.shape[1]
    slots = exports.shape[0]
    members = books.shape[3]
    nkz = G // zg
    nky = G // yg
    half_z = nkz // 2
    half = G // 2
    w, v = lax.axis_index("wide"), lax.axis_index("narrow")
    me = w * n_narrow + v
    my_z, my_y = lax.rem(me, zg), lax.div(me, zg)
    f32 = jnp.float32

    span = ranks // 2
    blocks = ranks // CHUNK
    cols = CHUNK * leaves
    levels = 2 if yg == 1 else 1
    low = nky // levels
    half_y = nky // 2
    strip = half_y // levels
    first_y = my_y * half_y

    half_j = half_z // 2

    def row_of(j, part):
        return j // half_j * SLOT + j % half_j * 3 + part

    barrier = pltpu.get_barrier_semaphore()

    def greet(at, column, to):
        pl.semaphore_signal(barrier, inc=1, device_id=to, device_id_type=pl.DeviceIdType.MESH)

    for far in (1, 0):
        each_peer(far, greet)

    arguments = [
        pltpu.make_async_copy(src, dst, loads.at[i])
        for i, (src, dst) in enumerate(
            (
                (leaf_cell_in, leaf_cell),
                (exports_in, exports),
                (tile_lists_in, tile_lists),
                (fraction_in, fraction),
                (masses_in, masses),
            )
        )
    ]
    for copy in arguments:
        copy.start()
    for copy in arguments:
        copy.wait()

    leaf_row = iota((leaves, members), 0)
    lane = iota((1, members), 1)
    for c, extent in enumerate((PX, PY, PZ)):
        cell = jnp.zeros((leaves, members), f32)
        for n in range(leaves):
            cell = jnp.where(leaf_row == n, leaf_cell[c, n].astype(f32), cell)
        u = jnp.concatenate(
            [fraction[c : c + 1, n * members : (n + 1) * members] for n in range(leaves)], axis=0
        )
        books[0, c] = cell + (u * (extent - 1.0) + 0.5)
    books[0, 3] = jnp.concatenate(
        [masses[:, n * members : (n + 1) * members] for n in range(leaves)], axis=0
    )
    lists = jnp.zeros((leaves, members), f32)
    for n in range(leaves):
        both = jnp.where(
            lane < members // 2, tile_lists[0, n].astype(f32), tile_lists[1, n].astype(f32)
        )
        lists = jnp.where(leaf_row == n, both, lists)
    books[0, 4] = lists

    particles = leaves * members
    patch_row = iota((AB, particles), 0)
    planar_weights = None
    for c, extent, index in ((0, PX, patch_row // PY), (1, PY, patch_row % PY)):
        coordinate = 0.5 + fraction[c : c + 1, :] * (extent - 1.0)
        part = jnp.maximum(0.0, 1.0 - jnp.abs(coordinate - (index.astype(f32) + 0.5)))
        planar_weights = part if planar_weights is None else planar_weights * part
    planar[...] = planar_weights
    coordinate = 0.5 + fraction[2:3, :] * (PZ - 1.0)
    deep = jnp.maximum(
        0.0, 1.0 - jnp.abs(coordinate - (iota((PZ, particles), 0).astype(f32) + 0.5))
    )
    deep_hi, deep_lo = split(deep)
    wz_hi[...] = jnp.zeros_like(wz_hi)
    wz_lo[...] = jnp.zeros_like(wz_lo)
    for n in range(leaves):
        at = slice(n * members, (n + 1) * members)
        wz_hi[n * PZ : (n + 1) * PZ, at] = deep_hi[:, at]
        wz_lo[n * PZ : (n + 1) * PZ, at] = deep_lo[:, at]
    weighted = split(jnp.concatenate([planar_weights * masses[...]] * leaves, axis=0))
    width = leaves * PZ
    lone = leaves * AB
    patches = dot3((wz_hi[...], wz_lo[...]), weighted, ((1,), (1,)))
    same = iota((width, lone), 0) // PZ == iota((width, lone), 1) // AB
    patches = jnp.where(same, patches, 0.0)
    empty = jnp.zeros_like(patches)
    patches = split(
        jnp.concatenate(
            [
                jnp.concatenate([patches, empty], axis=1),
                jnp.concatenate([empty, patches], axis=1),
            ],
            axis=0,
        )
    )

    column = iota((1, width), 1)
    place = (column % PZ).astype(f32)
    note = jnp.zeros((1, 2 * lone), f32)
    for n in range(leaves):
        place = jnp.where(column // PZ == n, place + leaf_cell[2, n].astype(f32), place)
        for c in range(2):
            note = jnp.where(
                iota((1, 2 * lone), 1) // AB == c * leaves + n, leaf_cell[c, n].astype(f32), note
            )
    alternate = 1.0 - 2.0 * (place.astype(jnp.int32) & 1).astype(f32)
    row = iota((zg * SLOT, 1), 0)
    wave = row % half_z * zg + row // SLOT
    c, s = sincos(wave.astype(f32) * place)
    s = jnp.where(wave == 0, alternate, s)
    flat = dot3(split(jnp.concatenate([c, s], axis=1)), patches)
    zt[...] = jnp.where(row % SLOT == half_z, note, flat)

    def own(n, carry):
        pair_job(n, 0, n, leaf_cell, books, forces)
        return carry

    sooner = leaves // 4
    lax.fori_loop(0, sooner, own, 0)
    pl.semaphore_wait(barrier, ranks - 1)

    for far in (1, 0):

        def send_out(at, column, to):
            group = lax.rem(at * n_narrow + column, zg)
            remote(
                zt.at[pl.ds(pl.multiple_of(group * SLOT, SLOT), half_z + 1), :],
                recv.at[pl.ds(pl.multiple_of(place_of(far, w, v) * SLOT, SLOT), half_z + 1), :],
                sends.at[far],
                recvs.at[far],
                to,
            ).start()

        each_peer(far, send_out)
    near = []
    for face, to in enumerate(
        (
            {"wide": lax.rem(w + n_wide - 1, n_wide), "narrow": v},
            {"wide": lax.rem(w + 1, n_wide), "narrow": v},
            {"wide": w, "narrow": lax.rem(v + n_narrow - 1, n_narrow)},
            {"wide": w, "narrow": lax.rem(v + 1, n_narrow)},
        )
    ):
        near.append(
            remote(books.at[0], books.at[face + 1], near_send.at[face], near_recv.at[face], to)
        )
    for copy in near:
        copy.start()

    recv[pl.ds(pl.multiple_of(place_of(0, w, v) * SLOT, SLOT), SLOT), :] = zt[
        pl.ds(pl.multiple_of(my_z * SLOT, SLOT), SLOT), :
    ]

    row = iota((half, 1), 0)
    wave = row
    c, s = sincos(wave.astype(f32) * place)
    tilt = slope(wave)
    psi = split(tilt * s) + split(-(tilt * c))
    s = jnp.where(wave == 0, alternate, s)
    for i, table in enumerate(split(c) + split(s)):
        for step in range(half_z):
            at = (2 * step + i // 2) * zg
            basis[i % 2, at : at + zg, :] = table[step * zg : (step + 1) * zg, :]
    for i, table in enumerate(psi):
        lone_basis[i] = table

    unit = 2.0 * math.pi / G
    wave_x, _ = real_mode(iota((1, G), 1), G)
    index_y = iota((nky, 1), 0)
    wave_y = first_y + index_y // (2 * strip) * strip + index_y % strip
    wave_y = jnp.where((wave_y == 0) & (index_y % (2 * strip) >= strip), half, wave_y)
    kx = wave_x.astype(f32) * unit
    ky = wave_y.astype(f32) * unit
    plane = kx * kx + ky * ky
    top = jnp.exp(-plane * (SCREEN * SCREEN)) * (share(wave_x) * share(wave_y))

    def fill_green(j, carry):
        wave_z = jnp.full((1, 1), lax.rem(j, half_z) * zg + my_z, jnp.int32)
        wave_z = jnp.where((wave_z == 0) & (j >= half_z), half, wave_z)
        kz = wave_z.astype(f32) * unit
        kz2 = kz * kz
        scale = jnp.exp(-kz2 * (SCREEN * SCREEN)) * share(wave_z) * (-4.0 * math.pi / G**3)
        total = plane + kz2
        green[j] = jnp.where(total > 0, top * scale / jnp.where(total > 0, total, 1.0), 0.0)
        return carry

    lax.fori_loop(0, half_z + 1, fill_green, 0)

    lax.fori_loop(sooner, leaves, own, 0)

    def received(far, at, buffer, rows):
        whole = buffer.at[pl.ds(0, (span - 1 + far) * rows), :]
        return remote(
            whole,
            whole,
            sends.at[at + far],
            recvs.at[at + far],
            {"wide": lax.rem(w + 1, n_wide), "narrow": v},
        )

    def gathered(block, j):
        turned = recv[pl.ds(block * CHUNK * SLOT + j, CHUNK, SLOT), :].T
        return [
            jnp.concatenate(
                [
                    turned[part * lone + n * AB : part * lone + (n + 1) * AB, :]
                    for n in range(leaves)
                ],
                axis=1,
            )
            for part in range(2)
        ]

    def tables(block):
        place_x, place_y = gathered(block, half_z)
        value, tilt = axis_tables(place_x[0:1, :], half, 0, PX)
        for a in range(PX):
            for kind, table in enumerate((value[a], tilt[a])):
                at = slice((kind * PX + a) * cols, (kind * PX + a + 1) * cols)
                for part in range(2):
                    hi, lo = split(table[part])
                    ee_hi[block, part * half : (part + 1) * half, at] = hi
                    ee_lo[block, part * half : (part + 1) * half, at] = lo
        value, tilt = axis_tables(place_y[0:1, :], half_y, first_y, PY)
        for b in range(PY):
            for kind, table in enumerate((value[b], tilt[b])):
                for level in range(levels):
                    for part in range(2):
                        at = (2 * level + part) * strip
                        rows = table[part][level * strip : (level + 1) * strip, :]
                        exact[block, kind * PY + b, at : at + strip, :] = rows
                        short_tables[block, kind * PY + b, at : at + strip, :] = rows.astype(
                            jnp.bfloat16
                        )

    def mixed(rows, block, table, first, last):
        halves = []
        for a in range(PX):
            m = None
            for b in range(PY):
                term = rows[a * PY + b : a * PY + b + 1, :] * table[block, b, first:last, :]
                m = term if m is None else m + term
            halves.append(m)
        return jnp.concatenate(halves, axis=1)

    nt = functools.partial(
        lax.dot_general,
        dimension_numbers=(((1,), (1,)), ((), ())),
        preferred_element_type=f32,
    )
    nn = functools.partial(jnp.dot, preferred_element_type=f32)

    def stacked(hi, lo, table_hi, table_lo, dot):
        if lo is None:
            return dot(hi, table_hi)
        rows, extra = hi.shape[0], lo.shape[0]
        both = dot(jnp.concatenate([hi, lo], axis=0), table_hi)
        first = both[0:extra] + (both[rows:] + dot(hi[0:extra], table_lo))
        return first if extra == rows else jnp.concatenate([first, both[extra:rows]], axis=0)

    def mix(block, j, edge):
        parts = gathered(block, j)
        pieces, lo = [], None
        if edge:
            hi, lo = split(
                jnp.concatenate([mixed(p, block, exact, 0, edge) for p in parts], axis=0)
            )
            pieces.append(hi)
        if edge < nky:
            pieces += [
                mixed(p.astype(jnp.bfloat16), block, short_tables, edge, nky) for p in parts
            ]
        return jnp.concatenate(pieces, axis=0), lo

    def forward(block, put):
        at = slice(0, PX * cols)
        ready = mix(block, 0, edge_of(0))
        for j in range(half_z):
            edge = edge_of(j)
            q = stacked(*ready, ee_hi[block, :, at], ee_lo[block, :, at], nt)
            if j + 1 < half_z:
                ready = mix(block, j + 1, edge_of(j + 1))
            for part in range(2):
                for first, last in ((0, edge), (edge, nky)):
                    if first < last:
                        count = last - first
                        start = 2 * first + part * count
                        put(part * half_z + j, first, last, q[start : start + count])

    def contracted(u, block, table, first, last):
        found = []
        count = last - first
        for kind, bank in ((1, 0), (0, 1), (0, 0)):
            for a in range(PX):
                at = (kind * PX + a) * cols
                column = u[:, at : at + cols]
                for b in range(PY):
                    term = column * table[block, bank * PY + b, first:last, :]
                    step = 16
                    total = term[0:step]
                    for i in range(step, count, step):
                        total = total + term[i : i + step]
                    found.append(jnp.sum(total.astype(f32), axis=0, keepdims=True))
        return jnp.concatenate(found, axis=0)

    def fields_of(block, j, edge):
        def rows(buffer, first, last):
            return [buffer[part * half_z + j, first:last] for part in range(2) if first < last]

        hi = jnp.concatenate(rows(q_hi, 0, edge) + rows(q_hi, edge, nky), axis=0)
        lo = jnp.concatenate(rows(q_lo, 0, edge), axis=0) if edge else None
        return stacked(hi, lo, ee_hi[block], ee_lo[block], nn)

    def finish(block, j, edge, u):
        count = nky - edge
        alone = []
        for part in range(2):
            field = 0.0
            if edge:
                field = contracted(u[part * edge : (part + 1) * edge], block, exact, 0, edge)
            if count:
                start = 2 * edge + part * count
                field += contracted(
                    u[start : start + count].astype(jnp.bfloat16), block, short_tables, edge, nky
                )
            pair = jnp.concatenate(
                [field[0 : 2 * AB, n * CHUNK : (n + 1) * CHUNK] for n in range(leaves)], axis=0
            )
            alone += [field[2 * AB :, n * CHUNK : (n + 1) * CHUNK] for n in range(leaves)]
            msgs[pl.ds(block * CHUNK * BACK + row_of(j, part), CHUNK, BACK), :] = pair.T
        at = block * CHUNK * BACK + row_of(j, 2)
        msgs[pl.ds(at, CHUNK, BACK), :] = jnp.concatenate(alone, axis=0).T

    def send_back(far, stage):
        def send(at, column, to):
            place = pl.multiple_of(place_of(far, at, column) * BACK + stage * SLOT, SLOT)
            landing = pl.multiple_of(me * BACK + stage * SLOT, SLOT)
            remote(
                msgs.at[pl.ds(place, 3 * half_j), :],
                back.at[pl.ds(landing, 3 * half_j), :],
                sends.at[2 + 2 * stage + far],
                recvs.at[2 + 2 * stage + far],
                to,
            ).start()

        each_peer(far, send)

    def inverse(block, sent=None):
        order = list(reversed(range(half_z)))
        ready = fields_of(block, order[0], edge_of(order[0]))
        for i, j in enumerate(order):
            u = ready
            if i + 1 < half_z:
                ready = fields_of(block, order[i + 1], edge_of(order[i + 1]))
            finish(block, j, edge_of(j), u)
            if sent is not None and j % half_j == 0:
                send_back(sent, j // half_j)

    def edge_of(j):
        return low if j * zg < G // 8 else 0

    def begin(block):
        tables(block)

        def put(at, first, last, values):
            spectrum[at, first:last, :] = values

        forward(block, put)

    def go_on(block, carry):
        tables(block)

        def put(at, first, last, values):
            spectrum[at, first:last, :] += values

        forward(block, put)
        return carry

    def close(block):
        tables(block)

        def put(at, first, last, values):
            q = (spectrum[at, first:last, :] + values) * green[min(at, half_z) if at % half_z == 0 else at % half_z, first:last, :]
            if first < edge_of(at % half_z):
                q_hi[at, first:last, :], q_lo[at, first:last, :] = split(q)
            else:
                q_hi[at, first:last, :] = q.astype(jnp.bfloat16)

        forward(block, put)

    received(0, 0, recv, half_z + 1).wait_recv()
    begin(0)
    lax.fori_loop(1, blocks // 2, go_on, 0)
    received(1, 0, recv, half_z + 1).wait_recv()
    lax.fori_loop(blocks // 2, blocks - 1, go_on, 0)
    close(blocks - 1)

    for far in (1, 0):
        if blocks == 2:
            inverse(far, far)
        else:

            def back_block(block, carry):
                inverse(block)
                return carry

            lax.fori_loop(far * (blocks // 2), (far + 1) * (blocks // 2), back_block, 0)
            for stage in range(2):
                send_back(far, stage)
    back[pl.ds(pl.multiple_of(me * BACK, BACK), BACK), :] = msgs[
        pl.ds(pl.multiple_of(place_of(0, w, v) * BACK, BACK), BACK), :
    ]

    for copy in near:
        copy.wait_recv()

    def guest(j, carry):
        face = j // slots
        target = jnp.minimum(exports[j % slots, face], leaves - 1)
        pair_job(leaves + j, face + 1, target, leaf_cell, books, forces)
        return carry

    lax.fori_loop(0, 4 * slots, guest, 0)
    short = []
    for n in range(leaves):
        force = forces[n]
        for j in range(4 * slots):
            mine_too = jnp.where(exports[j % slots, j // slots] == n, 1.0, 0.0)
            force = force + forces[leaves + j] * mine_too
        short.append(force)
    short = jnp.concatenate(short, axis=1)

    for stage in range(2):
        for far in (0, 1):
            received(far, 2 + 2 * stage, back, 3 * half_j).wait_recv()

    def summed(j, part):
        total = back[pl.ds(row_of(j, part), zg, BACK), :]
        for h in range(1, yg):
            total = total + back[pl.ds(h * zg * BACK + row_of(j, part), zg, BACK), :]
        return total

    def own_part(table, start, rows):
        kept = jnp.where(column // PZ == 0, table[start : start + rows, :], 0.0)
        for n in range(1, leaves):
            at = start + n * rows
            kept = kept + jnp.where(column // PZ == n, table[at : at + rows, :], 0.0)
        return kept

    pairs = jnp.concatenate([summed(i // 2, i % 2) for i in range(nkz)], axis=0)
    along = dot3(split(pairs), (basis[0], basis[1]), ((0,), (0,)))
    lones = split(jnp.concatenate([summed(i, 2) for i in range(half_z)], axis=0))
    deep = None
    for part in range(2):
        rows = dot3(lones, (lone_basis[2 * part], lone_basis[2 * part + 1]), ((0,), (0,)))
        rows = own_part(rows, part * lone, AB)
        deep = rows if deep is None else deep + rows
    sampled = [own_part(along, 0, PZ), deep]
    sampled = jnp.concatenate(sampled, axis=0)
    got = dot3(split(sampled), (wz_hi[...], wz_lo[...]))
    for c in range(3):
        out[c : c + 1, :] = (
            jnp.sum(got[c * AB : (c + 1) * AB, :] * planar[...], axis=0, keepdims=True)
            + short[c : c + 1, :]
        )
    for copy in near:
        copy.wait_send()
    for far in range(2):
        received(far, 0, recv, half_z + 1).wait_send()
        for stage in range(2):
            received(far, 2 + 2 * stage, back, 3 * half_j).wait_send()


def local(fraction, masses, leaf_cell, exports, tile_lists):
    leaves = leaf_cell.shape[1]
    members = masses.shape[0] // leaves
    slots = exports.shape[1]
    ranks = lax.axis_size("wide") * lax.axis_size("narrow")
    f32, bf16 = jnp.float32, jnp.bfloat16
    zg = min(ranks, G // 8)
    yg = ranks // zg
    nkz, nky = G // zg, G // yg
    cols = CHUNK * leaves
    width = leaves * PZ
    blocks = ranks // CHUNK
    return pl.pallas_call(
        functools.partial(kernel, zg, yg),
        out_shape=pltpu.VMEM((3, leaves * members), f32),
        in_specs=[ANY] * 5,
        out_specs=VMEM,
        scratch_shapes=[
            pltpu.SMEM(leaf_cell.shape, jnp.int32),
            pltpu.SMEM((slots, exports.shape[0]), jnp.int32),
            pltpu.SMEM(tile_lists.shape, jnp.int32),
            pltpu.VMEM(fraction.shape, f32),
            pltpu.VMEM((1, leaves * members), f32),
            pltpu.SemaphoreType.DMA((5,)),
            pltpu.VMEM((zg * SLOT, width), f32),
            pltpu.VMEM((ranks * SLOT, width), f32),
            pltpu.VMEM((5, 5, leaves, members), f32),
            pltpu.VMEM((nkz // 2 + 1, nky, G), f32),
            pltpu.VMEM((blocks, G, 2 * PX * cols), bf16),
            pltpu.VMEM((blocks, G, 2 * PX * cols), bf16),
            pltpu.VMEM((blocks, 2 * PY, nky, cols), f32),
            pltpu.VMEM((blocks, 2 * PY, nky, cols), bf16),
            pltpu.VMEM((nkz, nky, G), f32),
            pltpu.VMEM((nkz, nky, G), bf16),
            pltpu.VMEM((nkz, nky, G), bf16),
            pltpu.VMEM((ranks * BACK, width), f32),
            pltpu.VMEM((ranks * BACK, width), f32),
            pltpu.VMEM((leaves + 4 * slots, 8, members), f32),
            pltpu.VMEM((width, leaves * members), bf16),
            pltpu.VMEM((width, leaves * members), bf16),
            pltpu.VMEM((2, G, width), bf16),
            pltpu.VMEM((4, G // 2, width), bf16),
            pltpu.VMEM((AB, leaves * members), f32),
            pltpu.SemaphoreType.DMA((4,)),
            pltpu.SemaphoreType.DMA((4,)),
            pltpu.SemaphoreType.DMA((6,)),
            pltpu.SemaphoreType.DMA((6,)),
        ],
        compiler_params=pltpu.CompilerParams(
            collective_id=0, has_side_effects=True, vmem_limit_bytes=56 * 2**20
        ),
        name="treepm",
    )(leaf_cell, exports.T, tile_lists, fraction, masses.reshape(1, -1))


def solution(mesh):
    placed = (
        P(None, ("wide", "narrow")),
        P(("wide", "narrow")),
        P(None, ("wide", "narrow")),
        P(None, ("wide", "narrow")),
        P(None, ("wide", "narrow")),
    )
    return jax.shard_map(
        local, mesh=mesh, in_specs=placed, out_specs=P(None, ("wide", "narrow")), check_vma=False
    )
```

```python
import functools
import math

import jax
import jax.numpy as jnp
from jax import lax
from jax.experimental import pallas as pl
from jax.experimental.pallas import tpu as pltpu
from jax.sharding import PartitionSpec as P

G = 256
PX = 2
PY = 4
PZ = 16
AB = PX * PY
SLOT = 8
BACK = 16
CHUNK = 16
SCREEN = 0.5
SOFTEN = 0.5
ERFCX = (
    0.2820947416810428,
    0.28210427504184366,
    0.24651391069954823,
    0.18039116519942175,
    0.058372405908860704,
    0.0792320361696661,
    -0.1983246779625943,
    0.030722780905291756,
    0.06437369661731697,
    -0.025480486181070308,
)
VMEM = pl.BlockSpec(memory_space=pltpu.VMEM)
ANY = pl.BlockSpec(memory_space=pl.ANY)


def iota(shape, dim):
    return lax.broadcasted_iota(jnp.int32, shape, dim)


def sincos(count):
    quarters = count * (4.0 / G)
    near = jnp.floor(quarters + 0.5)
    z = (quarters - near) * (math.pi / 2)
    q = near.astype(jnp.int32)
    zz = z * z
    c = 1.0 + zz * (-0.5 + zz * (1.0 / 24 + zz * (-1.0 / 720 + zz * (1.0 / 40320))))
    s = z * (1.0 + zz * (-1.0 / 6 + zz * (1.0 / 120 + zz * (-1.0 / 5040))))
    swap = (q & 1) == 1
    cosine = jnp.where(swap, s, c)
    sine = jnp.where(swap, c, s)
    cosine = jnp.where(((q + 1) & 2) == 2, -cosine, cosine)
    sine = jnp.where((q & 2) == 2, -sine, sine)
    return cosine, sine


def split(x):
    hi = x.astype(jnp.bfloat16)
    return hi, (x - hi.astype(jnp.float32)).astype(jnp.bfloat16)


def dot3(left, right, dims=((1,), (0,))):
    dims = (dims, ((), ()))
    dot = functools.partial(
        lax.dot_general, dimension_numbers=dims, preferred_element_type=jnp.float32
    )
    return dot(left[0], right[0]) + (dot(left[0], right[1]) + dot(left[1], right[0]))


def slope(wave):
    w = wave.astype(jnp.float32)
    return (8.0 * sincos(w)[1] - sincos(2.0 * w)[1]) * (1.0 / 6.0)


def real_mode(index, count):
    half = count // 2
    wave = index // count * half + index % half
    second = (index % count) // half
    top = (second == 1) & (wave == 0)
    sine = (second == 1) & (wave > 0)
    return jnp.where(top, G // 2, wave), sine


def share(wave):
    return jnp.where(wave % (G // 2) == 0, 1.0, 2.0)


def each_peer(far, visit):
    n_wide, n_narrow = lax.axis_size("wide"), lax.axis_size("narrow")
    w, v = lax.axis_index("wide"), lax.axis_index("narrow")
    span = n_narrow // 2
    start = lax.rem(lax.div(v, span) + far, 2) * span
    columns = [start + lax.rem(lax.rem(v, span) + b, span) for b in range(span)]

    def row(at, first):
        for column in columns[first:]:
            visit(at, column, {"wide": at, "narrow": column})

    row(w, 1 - far)
    if n_wide <= 8:
        for a in range(1, n_wide):
            row(lax.rem(w + a, n_wide), 0)
    else:

        def step(a, carry):
            row(lax.rem(w + a, n_wide), 0)
            return carry

        lax.fori_loop(1, n_wide, step, 0)


def place_of(far, w, v):
    n_wide, n_narrow = lax.axis_size("wide"), lax.axis_size("narrow")
    span = n_narrow // 2
    return (far * n_wide + w) * span + lax.rem(v, span)


def remote(src, dst, send, recv, to):
    return pltpu.make_async_remote_copy(
        src_ref=src,
        dst_ref=dst,
        send_sem=send,
        recv_sem=recv,
        device_id=to,
        device_id_type=pl.DeviceIdType.MESH,
    )


def axis_tables(position, waves, first, steps):
    rows = waves
    row = iota((rows, 1), 0)
    wave = first + row
    c, s = sincos(wave.astype(jnp.float32) * position)
    turn_c, turn_s = sincos(wave.astype(jnp.float32))
    tilt = slope(wave)
    alternate = 1.0 - 2.0 * (position.astype(jnp.int32) & 1).astype(jnp.float32)
    top = wave == 0
    values, slopes = [], []
    for b in range(steps):
        if b:
            c, s = c * turn_c - s * turn_s, s * turn_c + c * turn_s
            alternate = -alternate
        values.append((c, jnp.where(top, alternate, s)))
        slopes.append((tilt * s, -(tilt * c)))
    return values, slopes


def pair_job(job, rank, target, leaf_cell, books, forces):
    members = books.shape[3]
    leaves = books.shape[2]
    leaf = iota((leaves, members), 0).astype(jnp.float32)
    lane = iota((1, members), 1)
    tgt = [books[0, c, pl.ds(target, 1), :] for c in range(3)]
    origin = [leaf_cell[c, target].astype(jnp.float32) for c in range(3)]
    lists = books[rank, 4, pl.ds(target, 1), :]
    swapped = pltpu.roll(lists, members // 2, 1)
    total = [0.0, 0.0, 0.0]
    for k in range(2):
        wanted = jnp.where((lane < members // 2) == (k == 0), lists, swapped)
        mine = leaf == wanted
        rows = []
        for c in range(4):
            row = jnp.sum(jnp.where(mine, books[rank, c], 0.0), axis=0, keepdims=True)
            if c < 3:
                row = row - G * jnp.floor((row - origin[c]) * (1.0 / G) + 0.5)
            rows.append(row)
        cols = jnp.concatenate(rows + [jnp.zeros((4, members), jnp.float32)], axis=0).T
        d = [
            jnp.broadcast_to(cols[:, c : c + 1], (members, members)) - tgt[c] for c in range(3)
        ]
        squared = d[0] * d[0] + d[1] * d[1] + d[2] * d[2]
        r = squared * lax.rsqrt(jnp.maximum(squared, 1e-30))
        t = lax.rsqrt(1.0 + 0.5 * r)
        t = t * t
        poly = ERFCX[-1] * t + ERFCX[-2]
        for coefficient in ERFCX[-3::-1]:
            poly = poly * t + coefficient
        screened = jnp.exp(-squared) * (poly * t + (2.0 / math.sqrt(math.pi)) * r)
        inv = lax.rsqrt(squared + SOFTEN * SOFTEN)
        w = cols[:, 3:4] * screened * (inv * inv * inv)
        for c in range(3):
            total[c] = total[c] + jnp.sum(w * d[c], axis=0, keepdims=True)
    forces[job] = jnp.concatenate(total + [jnp.zeros((5, members), jnp.float32)], axis=0)


def kernel(
    zg,
    yg,
    leaf_cell_in,
    exports_in,
    tile_lists_in,
    fraction_in,
    masses_in,
    out,
    leaf_cell,
    exports,
    tile_lists,
    fraction,
    masses,
    loads,
    zt,
    recv,
    books,
    green,
    ee_hi,
    ee_lo,
    exact,
    short_tables,
    spectrum,
    q_hi,
    q_lo,
    msgs,
    back,
    forces,
    wz_hi,
    wz_lo,
    basis,
    lone_basis,
    planar,
    near_send,
    near_recv,
    sends,
    recvs,
):
    n_wide, n_narrow = lax.axis_size("wide"), lax.axis_size("narrow")
    ranks = n_wide * n_narrow
    leaves = leaf_cell.shape[1]
    slots = exports.shape[0]
    members = books.shape[3]
    nkz = G // zg
    nky = G // yg
    half_z = nkz // 2
    half = G // 2
    w, v = lax.axis_index("wide"), lax.axis_index("narrow")
    me = w * n_narrow + v
    my_z, my_y = lax.rem(me, zg), lax.div(me, zg)
    f32 = jnp.float32

    span = ranks // 2
    blocks = ranks // CHUNK
    cols = CHUNK * leaves
    levels = 2 if yg == 1 else 1
    low = nky // levels
    half_y = nky // 2
    strip = half_y // levels
    first_y = my_y * half_y

    half_j = half_z // 2

    def row_of(j, part):
        return j // half_j * SLOT + j % half_j * 3 + part

    barrier = pltpu.get_barrier_semaphore()

    def greet(at, column, to):
        pl.semaphore_signal(barrier, inc=1, device_id=to, device_id_type=pl.DeviceIdType.MESH)

    for far in (1, 0):
        each_peer(far, greet)

    arguments = [
        pltpu.make_async_copy(src, dst, loads.at[i])
        for i, (src, dst) in enumerate(
            (
                (leaf_cell_in, leaf_cell),
                (exports_in, exports),
                (tile_lists_in, tile_lists),
                (fraction_in, fraction),
                (masses_in, masses),
            )
        )
    ]
    for copy in arguments:
        copy.start()
    for copy in arguments:
        copy.wait()

    leaf_row = iota((leaves, members), 0)
    lane = iota((1, members), 1)
    for c, extent in enumerate((PX, PY, PZ)):
        cell = jnp.zeros((leaves, members), f32)
        for n in range(leaves):
            cell = jnp.where(leaf_row == n, leaf_cell[c, n].astype(f32), cell)
        u = jnp.concatenate(
            [fraction[c : c + 1, n * members : (n + 1) * members] for n in range(leaves)], axis=0
        )
        books[0, c] = cell + (u * (extent - 1.0) + 0.5)
    books[0, 3] = jnp.concatenate(
        [masses[:, n * members : (n + 1) * members] for n in range(leaves)], axis=0
    )
    lists = jnp.zeros((leaves, members), f32)
    for n in range(leaves):
        both = jnp.where(
            lane < members // 2, tile_lists[0, n].astype(f32), tile_lists[1, n].astype(f32)
        )
        lists = jnp.where(leaf_row == n, both, lists)
    books[0, 4] = lists

    particles = leaves * members
    patch_row = iota((AB, particles), 0)
    planar_weights = None
    for c, extent, index in ((0, PX, patch_row // PY), (1, PY, patch_row % PY)):
        coordinate = 0.5 + fraction[c : c + 1, :] * (extent - 1.0)
        part = jnp.maximum(0.0, 1.0 - jnp.abs(coordinate - (index.astype(f32) + 0.5)))
        planar_weights = part if planar_weights is None else planar_weights * part
    planar[...] = planar_weights
    coordinate = 0.5 + fraction[2:3, :] * (PZ - 1.0)
    deep = jnp.maximum(
        0.0, 1.0 - jnp.abs(coordinate - (iota((PZ, particles), 0).astype(f32) + 0.5))
    )
    deep_hi, deep_lo = split(deep)
    wz_hi[...] = jnp.zeros_like(wz_hi)
    wz_lo[...] = jnp.zeros_like(wz_lo)
    for n in range(leaves):
        at = slice(n * members, (n + 1) * members)
        wz_hi[n * PZ : (n + 1) * PZ, at] = deep_hi[:, at]
        wz_lo[n * PZ : (n + 1) * PZ, at] = deep_lo[:, at]
    weighted = split(jnp.concatenate([planar_weights * masses[...]] * leaves, axis=0))
    width = leaves * PZ
    lone = leaves * AB
    patches = dot3((wz_hi[...], wz_lo[...]), weighted, ((1,), (1,)))
    same = iota((width, lone), 0) // PZ == iota((width, lone), 1) // AB
    patches = jnp.where(same, patches, 0.0)
    empty = jnp.zeros_like(patches)
    patches = split(
        jnp.concatenate(
            [
                jnp.concatenate([patches, empty], axis=1),
                jnp.concatenate([empty, patches], axis=1),
            ],
            axis=0,
        )
    )

    column = iota((1, width), 1)
    place = (column % PZ).astype(f32)
    note = jnp.zeros((1, 2 * lone), f32)
    for n in range(leaves):
        place = jnp.where(column // PZ == n, place + leaf_cell[2, n].astype(f32), place)
        for c in range(2):
            note = jnp.where(
                iota((1, 2 * lone), 1) // AB == c * leaves + n, leaf_cell[c, n].astype(f32), note
            )
    alternate = 1.0 - 2.0 * (place.astype(jnp.int32) & 1).astype(f32)
    row = iota((zg * SLOT, 1), 0)
    wave = row % half_z * zg + row // SLOT
    c, s = sincos(wave.astype(f32) * place)
    s = jnp.where(wave == 0, alternate, s)
    flat = dot3(split(jnp.concatenate([c, s], axis=1)), patches)
    zt[...] = jnp.where(row % SLOT == half_z, note, flat)

    def own(n, carry):
        pair_job(n, 0, n, leaf_cell, books, forces)
        return carry

    sooner = leaves // 4
    lax.fori_loop(0, sooner, own, 0)
    pl.semaphore_wait(barrier, ranks - 1)

    for far in (1, 0):

        def send_out(at, column, to):
            group = lax.rem(at * n_narrow + column, zg)
            remote(
                zt.at[pl.ds(pl.multiple_of(group * SLOT, SLOT), half_z + 1), :],
                recv.at[pl.ds(pl.multiple_of(place_of(far, w, v) * SLOT, SLOT), half_z + 1), :],
                sends.at[far],
                recvs.at[far],
                to,
            ).start()

        each_peer(far, send_out)
    near = []
    for face, to in enumerate(
        (
            {"wide": lax.rem(w + n_wide - 1, n_wide), "narrow": v},
            {"wide": lax.rem(w + 1, n_wide), "narrow": v},
            {"wide": w, "narrow": lax.rem(v + n_narrow - 1, n_narrow)},
            {"wide": w, "narrow": lax.rem(v + 1, n_narrow)},
        )
    ):
        near.append(
            remote(books.at[0], books.at[face + 1], near_send.at[face], near_recv.at[face], to)
        )
    for copy in near:
        copy.start()

    recv[pl.ds(pl.multiple_of(place_of(0, w, v) * SLOT, SLOT), SLOT), :] = zt[
        pl.ds(pl.multiple_of(my_z * SLOT, SLOT), SLOT), :
    ]

    row = iota((half, 1), 0)
    wave = row
    c, s = sincos(wave.astype(f32) * place)
    tilt = slope(wave)
    psi = split(tilt * s) + split(-(tilt * c))
    s = jnp.where(wave == 0, alternate, s)
    for i, table in enumerate(split(c) + split(s)):
        for step in range(half_z):
            at = (2 * step + i // 2) * zg
            basis[i % 2, at : at + zg, :] = table[step * zg : (step + 1) * zg, :]
    for i, table in enumerate(psi):
        lone_basis[i % 2, :, i // 2 * width : (i // 2 + 1) * width] = table

    unit = 2.0 * math.pi / G
    wave_x, _ = real_mode(iota((1, G), 1), G)
    index_y = iota((nky, 1), 0)
    wave_y = first_y + index_y // (2 * strip) * strip + index_y % strip
    wave_y = jnp.where((wave_y == 0) & (index_y % (2 * strip) >= strip), half, wave_y)
    kx = wave_x.astype(f32) * unit
    ky = wave_y.astype(f32) * unit
    plane = kx * kx + ky * ky
    top = jnp.exp(-plane * (SCREEN * SCREEN)) * (share(wave_x) * share(wave_y))

    def fill_green(j, carry):
        wave_z = jnp.full((1, 1), lax.rem(j, half_z) * zg + my_z, jnp.int32)
        wave_z = jnp.where((wave_z == 0) & (j >= half_z), half, wave_z)
        kz = wave_z.astype(f32) * unit
        kz2 = kz * kz
        scale = jnp.exp(-kz2 * (SCREEN * SCREEN)) * share(wave_z) * (-4.0 * math.pi / G**3)
        total = plane + kz2
        green[j] = jnp.where(total > 0, top * scale / jnp.where(total > 0, total, 1.0), 0.0)
        return carry

    lax.fori_loop(0, half_z + 1, fill_green, 0)

    lax.fori_loop(sooner, leaves, own, 0)

    def received(far, at, buffer, rows):
        whole = buffer.at[pl.ds(0, (span - 1 + far) * rows), :]
        return remote(
            whole,
            whole,
            sends.at[at + far],
            recvs.at[at + far],
            {"wide": lax.rem(w + 1, n_wide), "narrow": v},
        )

    def gathered(block, j):
        turned = recv[pl.ds(block * CHUNK * SLOT + j, CHUNK, SLOT), :].T
        return [
            jnp.concatenate(
                [
                    turned[part * lone + n * AB : part * lone + (n + 1) * AB, :]
                    for n in range(leaves)
                ],
                axis=1,
            )
            for part in range(2)
        ]

    def tables(block):
        place_x, place_y = gathered(block, half_z)
        value, tilt = axis_tables(place_x[0:1, :], half, 0, PX)
        for a in range(PX):
            for kind, table in enumerate((value[a], tilt[a])):
                at = slice((kind * PX + a) * cols, (kind * PX + a + 1) * cols)
                for part in range(2):
                    hi, lo = split(table[part])
                    ee_hi[block, part * half : (part + 1) * half, at] = hi
                    ee_lo[block, part * half : (part + 1) * half, at] = lo
        value, tilt = axis_tables(place_y[0:1, :], half_y, first_y, PY)
        for b in range(PY):
            for kind, table in enumerate((value[b], tilt[b])):
                for level in range(levels):
                    for part in range(2):
                        at = (2 * level + part) * strip
                        rows = table[part][level * strip : (level + 1) * strip, :]
                        exact[block, kind * PY + b, at : at + strip, :] = rows
                        short_tables[block, kind * PY + b, at : at + strip, :] = rows.astype(
                            jnp.bfloat16
                        )

    def mixed(rows, block, table, first, last):
        halves = []
        for a in range(PX):
            m = None
            for b in range(PY):
                term = rows[a * PY + b : a * PY + b + 1, :] * table[block, b, first:last, :]
                m = term if m is None else m + term
            halves.append(m)
        return jnp.concatenate(halves, axis=1)

    nt = functools.partial(
        lax.dot_general,
        dimension_numbers=(((1,), (1,)), ((), ())),
        preferred_element_type=f32,
    )
    nn = functools.partial(jnp.dot, preferred_element_type=f32)

    def stacked(hi, lo, table_hi, table_lo, dot):
        if lo is None:
            return dot(hi, table_hi)
        rows, extra = hi.shape[0], lo.shape[0]
        both = dot(jnp.concatenate([hi, lo], axis=0), table_hi)
        first = both[0:extra] + (both[rows:] + dot(hi[0:extra], table_lo))
        return first if extra == rows else jnp.concatenate([first, both[extra:rows]], axis=0)

    def mix(block, j, edge):
        parts = gathered(block, j)
        pieces, lo = [], None
        if edge:
            hi, lo = split(
                jnp.concatenate([mixed(p, block, exact, 0, edge) for p in parts], axis=0)
            )
            pieces.append(hi)
        if edge < nky:
            pieces += [
                mixed(p.astype(jnp.bfloat16), block, short_tables, edge, nky) for p in parts
            ]
        return jnp.concatenate(pieces, axis=0), lo

    def forward(block, put):
        at = slice(0, PX * cols)
        ready = mix(block, 0, edge_of(0))
        for j in range(half_z):
            edge = edge_of(j)
            q = stacked(*ready, ee_hi[block, :, at], ee_lo[block, :, at], nt)
            if j + 1 < half_z:
                ready = mix(block, j + 1, edge_of(j + 1))
            for part in range(2):
                for first, last in ((0, edge), (edge, nky)):
                    if first < last:
                        count = last - first
                        start = 2 * first + part * count
                        put(part * half_z + j, first, last, q[start : start + count])

    def contracted(u, block, table, first, last):
        found = []
        count = last - first
        for kind, bank in ((1, 0), (0, 1), (0, 0)):
            for a in range(PX):
                at = (kind * PX + a) * cols
                column = u[:, at : at + cols]
                for b in range(PY):
                    term = column * table[block, bank * PY + b, first:last, :]
                    step = 16
                    total = term[0:step]
                    for i in range(step, count, step):
                        total = total + term[i : i + step]
                    found.append(jnp.sum(total.astype(f32), axis=0, keepdims=True))
        return jnp.concatenate(found, axis=0)

    def fields_of(block, j, edge):
        def rows(buffer, first, last):
            return [buffer[part * half_z + j, first:last] for part in range(2) if first < last]

        hi = jnp.concatenate(rows(q_hi, 0, edge) + rows(q_hi, edge, nky), axis=0)
        lo = jnp.concatenate(rows(q_lo, 0, edge), axis=0) if edge else None
        return stacked(hi, lo, ee_hi[block], ee_lo[block], nn)

    def finish(block, j, edge, u):
        count = nky - edge
        alone = []
        for part in range(2):
            field = 0.0
            if edge:
                field = contracted(u[part * edge : (part + 1) * edge], block, exact, 0, edge)
            if count:
                start = 2 * edge + part * count
                field += contracted(
                    u[start : start + count].astype(jnp.bfloat16), block, short_tables, edge, nky
                )
            pair = jnp.concatenate(
                [field[0 : 2 * AB, n * CHUNK : (n + 1) * CHUNK] for n in range(leaves)], axis=0
            )
            alone += [field[2 * AB :, n * CHUNK : (n + 1) * CHUNK] for n in range(leaves)]
            msgs[pl.ds(block * CHUNK * BACK + row_of(j, part), CHUNK, BACK), :] = pair.T
        at = block * CHUNK * BACK + row_of(j, 2)
        msgs[pl.ds(at, CHUNK, BACK), :] = jnp.concatenate(alone, axis=0).T

    def send_back(far, stage):
        def send(at, column, to):
            place = pl.multiple_of(place_of(far, at, column) * BACK + stage * SLOT, SLOT)
            landing = pl.multiple_of(me * BACK + stage * SLOT, SLOT)
            remote(
                msgs.at[pl.ds(place, 3 * half_j), :],
                back.at[pl.ds(landing, 3 * half_j), :],
                sends.at[2 + 2 * stage + far],
                recvs.at[2 + 2 * stage + far],
                to,
            ).start()

        each_peer(far, send)

    def inverse(block, sent=None):
        order = list(reversed(range(half_z)))
        ready = fields_of(block, order[0], edge_of(order[0]))
        for i, j in enumerate(order):
            u = ready
            if i + 1 < half_z:
                ready = fields_of(block, order[i + 1], edge_of(order[i + 1]))
            finish(block, j, edge_of(j), u)
            if sent is not None and j % half_j == 0:
                send_back(sent, j // half_j)

    def edge_of(j):
        return low if j * zg < G // 8 else 0

    def begin(block):
        tables(block)

        def put(at, first, last, values):
            spectrum[at, first:last, :] = values

        forward(block, put)

    def go_on(block, carry):
        tables(block)

        def put(at, first, last, values):
            spectrum[at, first:last, :] += values

        forward(block, put)
        return carry

    def close(block):
        tables(block)

        def put(at, first, last, values):
            q = (spectrum[at, first:last, :] + values) * green[min(at, half_z) if at % half_z == 0 else at % half_z, first:last, :]
            if first < edge_of(at % half_z):
                q_hi[at, first:last, :], q_lo[at, first:last, :] = split(q)
            else:
                q_hi[at, first:last, :] = q.astype(jnp.bfloat16)

        forward(block, put)

    received(0, 0, recv, half_z + 1).wait_recv()
    begin(0)
    lax.fori_loop(1, blocks // 2, go_on, 0)
    received(1, 0, recv, half_z + 1).wait_recv()
    lax.fori_loop(blocks // 2, blocks - 1, go_on, 0)
    close(blocks - 1)

    for far in (1, 0):
        if blocks == 2:
            inverse(far, far)
        else:

            def back_block(block, carry):
                inverse(block)
                return carry

            lax.fori_loop(far * (blocks // 2), (far + 1) * (blocks // 2), back_block, 0)
            for stage in range(2):
                send_back(far, stage)
    back[pl.ds(pl.multiple_of(me * BACK, BACK), BACK), :] = msgs[
        pl.ds(pl.multiple_of(place_of(0, w, v) * BACK, BACK), BACK), :
    ]

    for copy in near:
        copy.wait_recv()

    def guest(j, carry):
        face = j // slots
        target = jnp.minimum(exports[j % slots, face], leaves - 1)
        pair_job(leaves + j, face + 1, target, leaf_cell, books, forces)
        return carry

    lax.fori_loop(0, 4 * slots, guest, 0)
    short = []
    for n in range(leaves):
        force = forces[n]
        for j in range(4 * slots):
            mine_too = jnp.where(exports[j % slots, j // slots] == n, 1.0, 0.0)
            force = force + forces[leaves + j] * mine_too
        short.append(force)
    short = jnp.concatenate(short, axis=1)

    for stage in range(2):
        for far in (0, 1):
            received(far, 2 + 2 * stage, back, 3 * half_j).wait_recv()

    def summed(j, part):
        total = back[pl.ds(row_of(j, part), zg, BACK), :]
        for h in range(1, yg):
            total = total + back[pl.ds(h * zg * BACK + row_of(j, part), zg, BACK), :]
        return total

    def own_part(table, start, rows):
        kept = jnp.where(column // PZ == 0, table[start : start + rows, :], 0.0)
        for n in range(1, leaves):
            at = start + n * rows
            kept = kept + jnp.where(column // PZ == n, table[at : at + rows, :], 0.0)
        return kept

    pairs = jnp.concatenate([summed(i // 2, i % 2) for i in range(nkz)], axis=0)
    tn = functools.partial(
        lax.dot_general,
        dimension_numbers=(((0,), (0,)), ((), ())),
        preferred_element_type=f32,
    )

    def turned(values, table_hi, table_lo):
        hi, lo = split(values)
        both = tn(jnp.concatenate([hi, lo], axis=1), table_hi)
        return both[0:width] + (both[width:] + tn(hi, table_lo))

    along = turned(pairs, basis[0], basis[1])
    lones = jnp.concatenate([summed(i, 2) for i in range(half_z)], axis=0)
    rows = turned(lones, lone_basis[0], lone_basis[1])
    deep = own_part(rows[:, 0:width], 0, AB) + own_part(rows[:, width:], lone, AB)
    sampled = [own_part(along, 0, PZ), deep]
    sampled = jnp.concatenate(sampled, axis=0)
    got = stacked(*split(sampled), wz_hi[...], wz_lo[...], nn)
    for c in range(3):
        out[c : c + 1, :] = (
            jnp.sum(got[c * AB : (c + 1) * AB, :] * planar[...], axis=0, keepdims=True)
            + short[c : c + 1, :]
        )
    for copy in near:
        copy.wait_send()
    for far in range(2):
        received(far, 0, recv, half_z + 1).wait_send()
        for stage in range(2):
            received(far, 2 + 2 * stage, back, 3 * half_j).wait_send()


def local(fraction, masses, leaf_cell, exports, tile_lists):
    leaves = leaf_cell.shape[1]
    members = masses.shape[0] // leaves
    slots = exports.shape[1]
    ranks = lax.axis_size("wide") * lax.axis_size("narrow")
    f32, bf16 = jnp.float32, jnp.bfloat16
    zg = min(ranks, G // 8)
    yg = ranks // zg
    nkz, nky = G // zg, G // yg
    cols = CHUNK * leaves
    width = leaves * PZ
    blocks = ranks // CHUNK
    return pl.pallas_call(
        functools.partial(kernel, zg, yg),
        out_shape=pltpu.VMEM((3, leaves * members), f32),
        in_specs=[ANY] * 5,
        out_specs=VMEM,
        scratch_shapes=[
            pltpu.SMEM(leaf_cell.shape, jnp.int32),
            pltpu.SMEM((slots, exports.shape[0]), jnp.int32),
            pltpu.SMEM(tile_lists.shape, jnp.int32),
            pltpu.VMEM(fraction.shape, f32),
            pltpu.VMEM((1, leaves * members), f32),
            pltpu.SemaphoreType.DMA((5,)),
            pltpu.VMEM((zg * SLOT, width), f32),
            pltpu.VMEM((ranks * SLOT, width), f32),
            pltpu.VMEM((5, 5, leaves, members), f32),
            pltpu.VMEM((nkz // 2 + 1, nky, G), f32),
            pltpu.VMEM((blocks, G, 2 * PX * cols), bf16),
            pltpu.VMEM((blocks, G, 2 * PX * cols), bf16),
            pltpu.VMEM((blocks, 2 * PY, nky, cols), f32),
            pltpu.VMEM((blocks, 2 * PY, nky, cols), bf16),
            pltpu.VMEM((nkz, nky, G), f32),
            pltpu.VMEM((nkz, nky, G), bf16),
            pltpu.VMEM((nkz, nky, G), bf16),
            pltpu.VMEM((ranks * BACK, width), f32),
            pltpu.VMEM((ranks * BACK, width), f32),
            pltpu.VMEM((leaves + 4 * slots, 8, members), f32),
            pltpu.VMEM((width, leaves * members), bf16),
            pltpu.VMEM((width, leaves * members), bf16),
            pltpu.VMEM((2, G, width), bf16),
            pltpu.VMEM((2, G // 2, 2 * width), bf16),
            pltpu.VMEM((AB, leaves * members), f32),
            pltpu.SemaphoreType.DMA((4,)),
            pltpu.SemaphoreType.DMA((4,)),
            pltpu.SemaphoreType.DMA((6,)),
            pltpu.SemaphoreType.DMA((6,)),
        ],
        compiler_params=pltpu.CompilerParams(
            collective_id=0, has_side_effects=True, vmem_limit_bytes=56 * 2**20
        ),
        name="treepm",
    )(leaf_cell, exports.T, tile_lists, fraction, masses.reshape(1, -1))


def solution(mesh):
    placed = (
        P(None, ("wide", "narrow")),
        P(("wide", "narrow")),
        P(None, ("wide", "narrow")),
        P(None, ("wide", "narrow")),
        P(None, ("wide", "narrow")),
    )
    return jax.shard_map(
        local, mesh=mesh, in_specs=placed, out_specs=P(None, ("wide", "narrow")), check_vma=False
    )
```
